32 devices in a mesh: col: 4 (over y, x), row: 8 (over z, core).
Axes of the slice: x: 2, y: 2, z: 4, core: 2. Of those that a mesh axis runs over, the one named last changes fastest.
Arguments:
- velocity: bfloat16 [4, 524288], P(None, ('col', 'row')), may hold values from -6 to 6
- pair_struct: int32 [4096], P(('col', 'row')), may hold values from 0 to 63
- pair_panel: int32 [4096], P(('col', 'row')), may hold values from 0 to 127
- pair_count: int32 [32], P(('col', 'row')), may hold values from 32 to 128, as said below
- mortar_coef: bfloat16 [4096, 128, 128], P(('col', 'row')), may hold values from -0.0625 to 0.0625
- bem_matrix: bfloat16 [32768, 32768], P('row', 'col'), may hold values from -0.03125 to 0.03125
- self_term: float32 [32768], P('row'), may hold values from 0.5 to 2
Outputs:
- pressure: bfloat16 [4, 32768], P(None, 'row')
- load: float32 [4, 524288], P(None, ('col', 'row'))
The draws below stay inside these ranges and needn't reach their ends.
Inputs may be any that keep to these rules, and one draw needn't show every extreme that they name: pair_struct numbers a structural block within the slot's own device. `pair_count`: some device has all its slots live.
All inputs are finite; a program needn't handle non-finite values.
Results may differ from the reference program's by a relative error of at most 0.005.
Values may be sent and summed in bfloat16 or wider, within the bound.
No kernel may reach another device: no remote copies, remote signals or barrier semaphores. Data moves between devices by JAX's collectives and lax.ppermute only.
A program may use at most 128 MiB of HBM per device.

```python
import math
import jax
import jax.numpy as jnp
import numpy as np
from jax import lax

BLK = 128
PANELS = 16384
LOADS = 4
PAIRS_DEV = 128
NBLK = 128
SBLK_DEV = 64
NODES = 262144
SLOTS = 4096
N_COL = 4
N_ROW = 8


def draw_pair_count(key, part):
    key_counts = jax.random.fold_in(key, 11)
    key_full = jax.random.fold_in(key, 12)
    counts = jax.random.randint(key_counts, (N_COL * N_ROW,), PAIRS_DEV // 4, PAIRS_DEV + 1)
    chosen = jax.random.randint(key_full, (), 0, N_COL * N_ROW)
    return jnp.where(jnp.arange(N_COL * N_ROW) == chosen, PAIRS_DEV, counts).astype(jnp.int32)


def plant(drawn, key, smallest, largest):
    longest = drawn.shape.index(max(drawn.shape))
    spots = []
    for shift in (0, 1):
        where = [jax.random.randint(jax.random.fold_in(key, axis), (), 0, length) for axis, length in enumerate(drawn.shape)]
        where[longest] = (where[longest] + shift) % drawn.shape[longest]
        spots.append(tuple(where))
    return drawn.at[spots[0]].set(smallest).at[spots[1]].set(largest)


def steps_of(stream_key, extent, cuts, smallest, top_value):
    def one(dim, parts):
        draws = jax.random.uniform(jax.random.fold_in(jax.random.fold_in(stream_key, 6), dim), (parts,), jnp.float32, smallest / len(cuts), top_value / len(cuts))
        return jnp.repeat(jnp.exp(draws), extent[dim] // parts).reshape((-1,) + (1,) * (len(extent) - dim - 1))

    level = one(*cuts[0])
    for cut in cuts[1:]:
        level = level * one(*cut)
    return level


def rank_table(count, skew):
    portions = [(1 << 20) // math.isqrt(rank ** skew) + 1 for rank in range(1, count + 1)]
    scale = 1 + sum(portions) // (1 << 30)
    return np.cumsum(np.array([max(1, weight // scale) for weight in portions]))


def skewed_ids(stream_key, dims, amount, slope):
    grid = rank_table(amount, slope)
    ticket = jax.random.randint(jax.random.fold_in(stream_key, 1), dims, 0, int(grid[amount - 1]))
    standing = jnp.searchsorted(jnp.asarray(grid, jnp.int32), ticket, side="right")
    return jax.random.permutation(jax.random.fold_in(stream_key, 2), amount)[standing].astype(jnp.int32)


def gaussian(stream_key, extent, width, most, split=(), kind=jnp.bfloat16):
    loudness = steps_of(stream_key, extent, split, -0.22, 0.18) if split else 1.0
    array = jax.random.normal(stream_key, extent, jnp.float32) * width * loudness
    return jnp.minimum(jnp.maximum(array, -most), most).astype(kind)


def setup_inputs(seed: int = 0) -> dict:
    splits = jax.random.split(jax.random.key(seed), 8)
    velocity = gaussian(splits[0], (LOADS, 2 * NODES), 1.0, 6.0, ((1, 32),))
    pair_struct = plant(jax.random.randint(splits[1], (SLOTS,), 0, SBLK_DEV), jax.random.fold_in(splits[1], 1), 0, SBLK_DEV - 1).astype(jnp.int32)
    pair_panel = plant(skewed_ids(splits[2], (SLOTS,), NBLK, 2), jax.random.fold_in(splits[2], 3), 0, NBLK - 1).astype(jnp.int32)
    pair_count = draw_pair_count(jax.random.fold_in(splits[7], 71), 0)
    mortar_coef = gaussian(splits[4], (SLOTS, BLK, BLK), (BLK * PAIRS_DEV // 2) ** -0.5, 0.0625, ((0, 32),))
    bem_matrix = gaussian(splits[5], (2 * PANELS, 2 * PANELS), (2 * PANELS) ** -0.5, 0.03125, ((0, 8), (1, 4)))
    self_term = jnp.clip(jnp.exp(math.log(2.0) - 1.3862944 * jax.random.uniform(splits[6], (2 * PANELS,), jnp.float32) ** steps_of(splits[6], (2 * PANELS,), ((0, 8),), -0.2, 0.2)), 0.5, 2.0)
    return {"velocity": velocity, "pair_struct": pair_struct, "pair_panel": pair_panel, "pair_count": pair_count, "mortar_coef": mortar_coef, "bem_matrix": bem_matrix, "self_term": self_term}


def reference(velocity, pair_struct, pair_panel, pair_count, mortar_coef, bem_matrix, self_term):
    devcount = N_COL * N_ROW
    vel_dev = velocity.reshape(LOADS, devcount, SBLK_DEV, 2 * BLK).transpose(1, 0, 2, 3)
    coef_dev = mortar_coef.reshape(devcount, PAIRS_DEV, BLK, BLK)
    struct_dev = pair_struct.reshape(devcount, PAIRS_DEV)
    panel_dev = pair_panel.reshape(devcount, PAIRS_DEV)
    slot_ids = jnp.arange(PAIRS_DEV, dtype=jnp.int32)

    def forward(total, items):
        vel_one, coef_one, struct_one, panel_one, count_one = items
        live_mask = slot_ids < count_one
        picked = jnp.take(vel_one, struct_one, axis=1).reshape(LOADS, PAIRS_DEV, BLK, 2)
        terms = jnp.einsum("qpn,cqnk->cqpk", coef_one.astype(jnp.float32), picked.astype(jnp.float32), precision=lax.Precision.HIGHEST)
        onehot = ((panel_one[:, None] == jnp.arange(NBLK, dtype=jnp.int32)[None, :]) & live_mask[:, None]).astype(jnp.float32)
        return total + jnp.einsum("qb,cqpk->cbpk", onehot, terms, precision=lax.Precision.HIGHEST), None

    start = jnp.zeros((LOADS, NBLK, BLK, 2), jnp.float32)
    total, unused = lax.scan(forward, start, (vel_dev, coef_dev, struct_dev, panel_dev, pair_count))
    xvec = total.reshape(LOADS, 2 * PANELS).astype(jnp.bfloat16)
    pressure = jnp.dot(xvec, bem_matrix.T, preferred_element_type=jnp.float32)
    pressure = (pressure + self_term[None, :] * xvec.astype(jnp.float32)).astype(jnp.bfloat16)
    panel_view = pressure.reshape(LOADS, NBLK, 2 * BLK)

    def backward(carry, items):
        coef_one, struct_one, panel_one, count_one = items
        live_mask = slot_ids < count_one
        took = jnp.take(panel_view, panel_one, axis=1).reshape(LOADS, PAIRS_DEV, BLK, 2)
        terms = jnp.einsum("qpn,cqpk->cqnk", coef_one.astype(jnp.float32), took.astype(jnp.float32), precision=lax.Precision.HIGHEST)
        onehot = ((struct_one[:, None] == jnp.arange(SBLK_DEV, dtype=jnp.int32)[None, :]) & live_mask[:, None]).astype(jnp.float32)
        return carry, jnp.einsum("qs,cqnk->csnk", onehot, terms, precision=lax.Precision.HIGHEST)

    unused2, loads_dev = lax.scan(backward, jnp.zeros((), jnp.float32), (coef_dev, struct_dev, panel_dev, pair_count))
    load = loads_dev.transpose(1, 0, 2, 3, 4).reshape(LOADS, 2 * NODES)
    return pressure, load
```

```python
import functools

import jax
import jax.numpy as jnp
from jax import lax
from jax.experimental import pallas as pl
from jax.experimental.pallas import tpu as pltpu
from jax.sharding import PartitionSpec as P


F32 = jnp.float32
BF16 = jnp.bfloat16
GROUP = 16
ROWS_TILE = 256
SLOTS_BEM = 5


def half_split(block, wide):
    src = lax.broadcasted_iota(jnp.int32, (wide, wide), 0)
    dst = lax.broadcasted_iota(jnp.int32, (wide, wide), 1)
    want = jnp.where(dst < block, 2 * dst, 2 * (dst - block) + 1)
    return jnp.where(src == want, 1.0, 0.0).astype(BF16)


def half_spread(block, part):
    src = lax.broadcasted_iota(jnp.int32, (block, 2 * block), 0)
    dst = lax.broadcasted_iota(jnp.int32, (block, 2 * block), 1)
    return jnp.where(dst == 2 * src + part, 1.0, 0.0).astype(BF16)


def unpack_parts(wide_rows, cases, block):
    nb = wide_rows.shape[0]
    both = jnp.concatenate([wide_rows, wide_rows], axis=1)
    flat = both.reshape(nb * 2 * cases, 2 * block).astype(BF16)
    out = jnp.dot(flat, half_split(block, 2 * block), preferred_element_type=F32)
    out = out.reshape(nb, 2 * cases, 2 * block)
    row = lax.broadcasted_iota(jnp.int32, (nb, 2 * cases, block), 1)
    return jnp.where(row < cases, out[:, :, :block], out[:, :, block:])


def forward_kernel(struct_ref, panel_ref, count_ref, vel_ref, coef_hbm, keep_ref, send_ref,
                   coef, vel, acc, sems):
    slots, block, _ = coef.shape
    cases = vel_ref.shape[0]
    nblk = vel.shape[0]
    chunks = slots // GROUP
    core = lax.rem(lax.axis_index("row"), 2)

    def fetch(i):
        part = pl.ds(i * GROUP, GROUP)
        return pltpu.make_async_copy(coef_hbm.at[part], coef.at[part], sems.at[i])

    for i in range(chunks):
        fetch(i).start()
    acc[...] = jnp.zeros_like(acc)
    wide = 2 * block
    rows = jnp.stack(
        [vel_ref[:, b * wide:(b + 1) * wide].astype(F32) for b in range(nblk)], axis=0
    )
    vel[...] = unpack_parts(rows, cases, block)
    count = count_ref[0]
    zero = jnp.zeros((2 * cases, block), F32)

    def group(i, carry):
        fetch(i).wait()
        base = i * GROUP
        outs = []
        for j in range(0, GROUP, 2):
            qa, qb = base + j, base + j + 1
            va = jnp.where(qa < count, vel[struct_ref[qa]], 0.0)
            vb = jnp.where(qb < count, vel[struct_ref[qb]], 0.0)
            lhs = jnp.concatenate(
                [jnp.concatenate([va, zero], axis=1), jnp.concatenate([zero, vb], axis=1)], axis=0
            ).astype(BF16)
            rhs = jnp.concatenate([coef[qa], coef[qb]], axis=1)
            outs.append(lax.dot_general(lhs, rhs, (((1,), (1,)), ((), ())),
                                        preferred_element_type=F32))
        for j in range(0, GROUP, 2):
            out = outs[j // 2]
            acc[panel_ref[base + j]] += out[:2 * cases]
            acc[panel_ref[base + j + 1]] += out[2 * cases:]
        return carry

    lax.fori_loop(0, chunks, group, 0)
    cols, half = keep_ref.shape[0], keep_ref.shape[1]
    for c in range(cols):
        keep_ref[c] = acc[pl.ds((2 * c + core) * half, half)]
        send_ref[c] = acc[pl.ds((2 * c + 1 - core) * half, half)]


def bem_kernel(xa_ref, xb_ref, self_ref, bem_hbm, out_ref, tiles, xrow, sems):
    half, rows8, block = xa_ref.shape
    cases = rows8 // 2
    rows, width = bem_hbm.shape
    tile = tiles.shape[1]
    steps = rows // tile
    ring = tiles.shape[0]
    row_id = lax.axis_index("row")
    core = lax.rem(row_id, 2)
    wide = 2 * block

    def fetch(i, slot):
        return pltpu.make_async_copy(
            bem_hbm.at[pl.ds(i * tile, tile)], tiles.at[slot], sems.at[slot])

    for i in range(min(ring - 1, steps)):
        fetch(i, i).start()
    parts = jnp.concatenate([xa_ref[...], xb_ref[...]], axis=0).astype(F32)
    flat = parts.reshape(2 * half * rows8, block).astype(BF16)
    even = jnp.dot(flat, half_spread(block, 0), preferred_element_type=F32)
    odd = jnp.dot(flat, half_spread(block, 1), preferred_element_type=F32)
    line = lax.broadcasted_iota(jnp.int32, even.shape, 0)
    both = jnp.where(lax.rem(line, rows8) < cases, even, odd)
    both = both.reshape(2 * half, rows8, wide)
    for j in range(half):
        first = jnp.where(core == 0, both[j], both[half + j])
        second = jnp.where(core == 0, both[half + j], both[j])
        xrow[:, j * wide:(j + 1) * wide] = first.astype(BF16)
        xrow[:, (half + j) * wide:(half + j + 1) * wide] = second.astype(BF16)

    def step(i, carry):
        slot = lax.rem(i, ring)
        fetch(i, slot).wait()

        @pl.when(i + ring - 1 < steps)
        def _():
            fetch(i + ring - 1, lax.rem(i + ring - 1, ring)).start()

        got = lax.dot_general(xrow[...], tiles[slot], (((1,), (1,)), ((), ())),
                              preferred_element_type=F32)
        out_ref[:, pl.ds(pl.multiple_of(i * tile, tile), tile)] = got[:cases] + got[cases:]
        return carry

    lax.fori_loop(0, steps, step, 0)
    start = row_id * rows
    @pl.when(start // width == lax.axis_index("col"))
    def _():
        offset = pl.multiple_of(lax.rem(start, width), rows)
        own = xrow[:, pl.ds(offset, rows)].astype(F32)
        out_ref[...] += self_ref[...] * (own[:cases] + own[cases:])


def pressure_kernel(count, *refs):
    terms, (out_ref, parts_ref) = refs[:count], refs[count:]
    total = terms[0][...]
    for t in terms[1:]:
        total = total + t[...]
    rounded = total.astype(BF16)
    out_ref[...] = rounded
    cases = out_ref.shape[0]
    nb, _, block = parts_ref.shape
    wide = 2 * block
    again = rounded.astype(F32)
    rows = jnp.stack([again[:, b * wide:(b + 1) * wide] for b in range(nb)], axis=0)
    parts_ref[...] = unpack_parts(rows, cases, block).astype(BF16)


def backward_kernel(mine, ranks, struct_ref, panel_ref, count_ref, coef, *refs):
    pieces, (out_ref, table, acc) = refs[:ranks], refs[ranks:]
    slots, block, _ = coef.shape
    nblk, rows8, _ = acc.shape
    cases = rows8 // 2
    wide = 2 * block
    count = count_ref[0]
    me = lax.axis_index("row")
    for k in range(ranks):
        per = pieces[k].shape[0]
        table[pl.ds((me ^ k) * per, per)] = pieces[k][...].astype(F32)
    acc[...] = jnp.zeros_like(acc)

    def group(i, carry):
        base = i * GROUP
        outs = []
        for j in range(0, GROUP, 2):
            qa, qb = base + j, base + j + 1
            pa = jnp.where(qa < count, table[panel_ref[qa]], 0.0)
            pb = jnp.where(qb < count, table[panel_ref[qb]], 0.0)
            lhs = jnp.concatenate([pa, pb], axis=0).astype(BF16)
            rhs = jnp.concatenate([coef[qa], coef[qb]], axis=1)
            outs.append(jnp.dot(lhs, rhs, preferred_element_type=F32))
        for j in range(0, GROUP, 2):
            out = outs[j // 2]
            acc[struct_ref[base + j]] += out[:rows8, :block]
            acc[struct_ref[base + j + 1]] += out[rows8:, block:]
        return carry

    lax.fori_loop(0, slots // GROUP, group, 0)
    rest = acc[...].reshape(nblk * rows8, block)
    even = odd = None
    spread0, spread1 = half_spread(block, 0), half_spread(block, 1)
    for level in range(3):
        piece = rest.astype(BF16)
        rest = rest - piece.astype(F32)
        e = jnp.dot(piece, spread0, preferred_element_type=F32)
        o = jnp.dot(piece, spread1, preferred_element_type=F32)
        even = e if even is None else even + e
        odd = o if odd is None else odd + o
    even = even.reshape(nblk, rows8, wide)
    odd = odd.reshape(nblk, rows8, wide)
    for b in range(nblk):
        out_ref[:, b * wide:(b + 1) * wide] = even[b, :cases] + odd[b, cases:]


def swap(value, axis, size, mask):
    return lax.ppermute(value, axis, [(i, i ^ mask) for i in range(size)])


def on_device(velocity, pair_struct, pair_panel, pair_count, mortar_coef, bem_matrix, self_term):
    cases = velocity.shape[0]
    slots, block, _ = mortar_coef.shape
    wide = 2 * block
    node_blocks = velocity.shape[1] // wide
    ncol, nrow = lax.axis_size("col"), lax.axis_size("row")
    rows, width = bem_matrix.shape
    panel_blocks = ncol * width // wide
    half = panel_blocks // (2 * ncol)
    rows8 = 2 * cases
    smem = pl.BlockSpec(memory_space=pltpu.SMEM)
    vmem = pl.BlockSpec(memory_space=pltpu.VMEM)
    hbm = pl.BlockSpec(memory_space=pl.ANY)
    col = lax.axis_index("col")

    keep, send = pl.pallas_call(
        forward_kernel,
        name="mortar_forward",
        out_shape=[jax.ShapeDtypeStruct((ncol, half, rows8, block), F32)] * 2,
        in_specs=[smem, smem, smem, vmem, hbm],
        out_specs=[vmem, vmem],
        scratch_shapes=[
            pltpu.VMEM((slots, block, block), BF16),
            pltpu.VMEM((node_blocks, rows8, block), F32),
            pltpu.VMEM((panel_blocks, rows8, block), F32),
            pltpu.SemaphoreType.DMA((slots // GROUP,)),
        ],
        compiler_params=pltpu.CompilerParams(vmem_limit_bytes=24 << 20),
    )(pair_struct, pair_panel, pair_count, velocity, mortar_coef)

    chip = keep + swap(send, "row", nrow, 1)

    def piece(k):
        return lax.dynamic_index_in_dim(chip, col ^ k, 0, keepdims=False)

    plane = piece(0)
    for got in [swap(piece(k).astype(BF16), "col", ncol, k) for k in range(1, ncol)]:
        plane = plane + got.astype(F32)
    sent = plane.astype(BF16)
    whole = plane
    for got in [swap(sent, "row", nrow, 2 * k) for k in range(1, nrow // 2)]:
        whole = whole + got.astype(F32)
    xa = whole.astype(BF16)
    xb = swap(xa, "row", nrow, 1)

    partial_value = pl.pallas_call(
        bem_kernel,
        name="bem_product",
        out_shape=jax.ShapeDtypeStruct((cases, rows), F32),
        in_specs=[vmem, vmem, vmem, hbm],
        out_specs=vmem,
        scratch_shapes=[
            pltpu.VMEM((SLOTS_BEM, min(rows, ROWS_TILE), width), BF16),
            pltpu.VMEM((rows8, width), BF16),
            pltpu.SemaphoreType.DMA((SLOTS_BEM,)),
        ],
        compiler_params=pltpu.CompilerParams(vmem_limit_bytes=40 << 20),
    )(xa, xb, self_term.reshape(1, rows), bem_matrix)

    terms = [partial_value] + [swap(partial_value, "col", ncol, k) for k in range(1, ncol)]
    pressure, parts = pl.pallas_call(
        functools.partial(pressure_kernel, ncol),
        name="pressure_sum",
        out_shape=[
            jax.ShapeDtypeStruct((cases, rows), BF16),
            jax.ShapeDtypeStruct((rows // wide, rows8, block), BF16),
        ],
        in_specs=[vmem] * ncol,
        out_specs=[vmem, vmem],
        compiler_params=pltpu.CompilerParams(vmem_limit_bytes=16 << 20),
    )(*terms)

    mine = [parts] + [swap(parts, "row", nrow, 2 * k) for k in range(1, nrow // 2)]
    pieces = []
    for got in mine:
        pieces.append(got)
        pieces.append(swap(got, "row", nrow, 1))

    load = pl.pallas_call(
        functools.partial(backward_kernel, None, nrow),
        name="mortar_backward",
        out_shape=jax.ShapeDtypeStruct((cases, node_blocks * wide), F32),
        in_specs=[smem, smem, smem, vmem] + [vmem] * nrow,
        out_specs=vmem,
        scratch_shapes=[
            pltpu.VMEM((panel_blocks, rows8, block), F32),
            pltpu.VMEM((node_blocks, rows8, block), F32),
        ],
        compiler_params=pltpu.CompilerParams(vmem_limit_bytes=24 << 20),
    )(pair_struct, pair_panel, pair_count, mortar_coef, *pieces)
    return (pressure, load)


def solution(mesh):
    placed = (
        P(None, ("col", "row")),
        P(("col", "row")),
        P(("col", "row")),
        P(("col", "row")),
        P(("col", "row"), None, None),
        P("row", "col"),
        P("row"),
    )
    return jax.shard_map(
        on_device,
        mesh=mesh,
        in_specs=placed,
        out_specs=(P(None, "row"), P(None, ("col", "row"))),
        check_vma=False,
    )
```

```python
import functools

import jax
import jax.numpy as jnp
from jax import lax
from jax.experimental import pallas as pl
from jax.experimental.pallas import tpu as pltpu
from jax.sharding import PartitionSpec as P


F32 = jnp.float32
BF16 = jnp.bfloat16
GROUP = 16
ROWS_TILE = 256
SLOTS_BEM = 5


def half_split(block, wide):
    src = lax.broadcasted_iota(jnp.int32, (wide, wide), 0)
    dst = lax.broadcasted_iota(jnp.int32, (wide, wide), 1)
    want = jnp.where(dst < block, 2 * dst, 2 * (dst - block) + 1)
    return jnp.where(src == want, 1.0, 0.0).astype(BF16)


def half_spread(block, part):
    src = lax.broadcasted_iota(jnp.int32, (block, 2 * block), 0)
    dst = lax.broadcasted_iota(jnp.int32, (block, 2 * block), 1)
    return jnp.where(dst == 2 * src + part, 1.0, 0.0).astype(BF16)


def unpack_parts(wide_rows, cases, block):
    nb = wide_rows.shape[0]
    both = jnp.concatenate([wide_rows, wide_rows], axis=1)
    flat = both.reshape(nb * 2 * cases, 2 * block).astype(BF16)
    out = jnp.dot(flat, half_split(block, 2 * block), preferred_element_type=F32)
    out = out.reshape(nb, 2 * cases, 2 * block)
    row = lax.broadcasted_iota(jnp.int32, (nb, 2 * cases, block), 1)
    return jnp.where(row < cases, out[:, :, :block], out[:, :, block:])


def forward_kernel(count_ref, struct_hbm, panel_hbm, vel_hbm, coef_hbm, keep_ref, send_ref,
                   coef, vel_ref, vel, acc, struct_ref, panel_ref, sems, small_sems):
    slots, block, _ = coef.shape
    cases = vel_ref.shape[0]
    nblk = vel.shape[0]
    chunks = slots // GROUP
    core = lax.rem(lax.axis_index("row"), 2)

    def fetch(i):
        part = pl.ds(i * GROUP, GROUP)
        return pltpu.make_async_copy(coef_hbm.at[part], coef.at[part], sems.at[i])

    small = [
        pltpu.make_async_copy(src, dst, small_sems.at[n])
        for n, (src, dst) in enumerate(
            [(vel_hbm, vel_ref), (struct_hbm, struct_ref), (panel_hbm, panel_ref)])
    ]
    for copy in small:
        copy.start()
    for i in range(chunks):
        fetch(i).start()
    acc[...] = jnp.zeros_like(acc)
    wide = 2 * block
    small[0].wait()
    rows = jnp.stack(
        [vel_ref[:, b * wide:(b + 1) * wide].astype(F32) for b in range(nblk)], axis=0
    )
    vel[...] = unpack_parts(rows, cases, block)
    for copy in small[1:]:
        copy.wait()
    count = count_ref[0]
    zero = jnp.zeros((2 * cases, block), F32)

    def group(i, carry):
        fetch(i).wait()
        base = i * GROUP
        outs = []
        for j in range(0, GROUP, 2):
            qa, qb = base + j, base + j + 1
            va = jnp.where(qa < count, vel[struct_ref[qa]], 0.0)
            vb = jnp.where(qb < count, vel[struct_ref[qb]], 0.0)
            lhs = jnp.concatenate(
                [jnp.concatenate([va, zero], axis=1), jnp.concatenate([zero, vb], axis=1)], axis=0
            ).astype(BF16)
            rhs = jnp.concatenate([coef[qa], coef[qb]], axis=1)
            outs.append(lax.dot_general(lhs, rhs, (((1,), (1,)), ((), ())),
                                        preferred_element_type=F32))
        for j in range(0, GROUP, 2):
            out = outs[j // 2]
            acc[panel_ref[base + j]] += out[:2 * cases]
            acc[panel_ref[base + j + 1]] += out[2 * cases:]
        return carry

    lax.fori_loop(0, chunks, group, 0)
    cols, half = keep_ref.shape[0], keep_ref.shape[1]
    for c in range(cols):
        keep_ref[c] = acc[pl.ds((2 * c + core) * half, half)]
        send_ref[c] = acc[pl.ds((2 * c + 1 - core) * half, half)]


def bem_kernel(xa_ref, xb_ref, self_hbm, bem_hbm, out_ref, tiles, xrow, self_ref, sems, self_sem):
    half, rows8, block = xa_ref.shape
    cases = rows8 // 2
    rows, width = bem_hbm.shape
    tile = tiles.shape[1]
    steps = rows // tile
    ring = tiles.shape[0]
    row_id = lax.axis_index("row")
    core = lax.rem(row_id, 2)
    wide = 2 * block

    def fetch(i, slot):
        return pltpu.make_async_copy(
            bem_hbm.at[pl.ds(i * tile, tile)], tiles.at[slot], sems.at[slot])

    self_copy = pltpu.make_async_copy(self_hbm, self_ref, self_sem)
    for i in range(min(ring - 1, steps)):
        fetch(i, i).start()
    self_copy.start()
    parts = jnp.concatenate([xa_ref[...], xb_ref[...]], axis=0).astype(F32)
    flat = parts.reshape(2 * half * rows8, block).astype(BF16)
    even = jnp.dot(flat, half_spread(block, 0), preferred_element_type=F32)
    odd = jnp.dot(flat, half_spread(block, 1), preferred_element_type=F32)
    line = lax.broadcasted_iota(jnp.int32, even.shape, 0)
    both = jnp.where(lax.rem(line, rows8) < cases, even, odd)
    both = both.reshape(2 * half, rows8, wide)
    for j in range(half):
        first = jnp.where(core == 0, both[j], both[half + j])
        second = jnp.where(core == 0, both[half + j], both[j])
        xrow[:, j * wide:(j + 1) * wide] = first.astype(BF16)
        xrow[:, (half + j) * wide:(half + j + 1) * wide] = second.astype(BF16)

    def step(i, carry):
        slot = lax.rem(i, ring)
        fetch(i, slot).wait()

        @pl.when(i + ring - 1 < steps)
        def _():
            fetch(i + ring - 1, lax.rem(i + ring - 1, ring)).start()

        got = lax.dot_general(xrow[...], tiles[slot], (((1,), (1,)), ((), ())),
                              preferred_element_type=F32)
        out_ref[:, pl.ds(pl.multiple_of(i * tile, tile), tile)] = got[:cases] + got[cases:]
        return carry

    lax.fori_loop(0, steps, step, 0)
    start = row_id * rows
    self_copy.wait()

    @pl.when(start // width == lax.axis_index("col"))
    def _():
        offset = pl.multiple_of(lax.rem(start, width), rows)
        own = xrow[:, pl.ds(offset, rows)].astype(F32)
        out_ref[...] += self_ref[...][None, :] * (own[:cases] + own[cases:])


def pressure_kernel(count, *refs):
    terms, (out_ref, parts_ref) = refs[:count], refs[count:]
    total = terms[0][...]
    for t in terms[1:]:
        total = total + t[...]
    rounded = total.astype(BF16)
    out_ref[...] = rounded
    cases = out_ref.shape[0]
    nb, _, block = parts_ref.shape
    wide = 2 * block
    again = rounded.astype(F32)
    rows = jnp.stack([again[:, b * wide:(b + 1) * wide] for b in range(nb)], axis=0)
    parts_ref[...] = unpack_parts(rows, cases, block).astype(BF16)


def backward_kernel(ranks, struct_ref, panel_ref, count_ref, coef, *refs):
    pieces, (out_ref, table, acc) = refs[:ranks], refs[ranks:]
    slots, block, _ = coef.shape
    nblk, rows8, _ = acc.shape
    cases = rows8 // 2
    wide = 2 * block
    me = lax.axis_index("row")
    for k in range(ranks):
        per = pieces[k].shape[0]
        table[pl.ds((me ^ k) * per, per)] = pieces[k][...].astype(F32)
    acc[...] = jnp.zeros_like(acc)
    count = count_ref[0]

    def group(i, carry):
        base = i * GROUP
        outs = []
        for j in range(0, GROUP, 2):
            qa, qb = base + j, base + j + 1
            pa = jnp.where(qa < count, table[panel_ref[qa]], 0.0)
            pb = jnp.where(qb < count, table[panel_ref[qb]], 0.0)
            lhs = jnp.concatenate([pa, pb], axis=0).astype(BF16)
            rhs = jnp.concatenate([coef[qa], coef[qb]], axis=1)
            outs.append(jnp.dot(lhs, rhs, preferred_element_type=F32))
        for j in range(0, GROUP, 2):
            out = outs[j // 2]
            acc[struct_ref[base + j]] += out[:rows8, :block]
            acc[struct_ref[base + j + 1]] += out[rows8:, block:]
        return carry

    lax.fori_loop(0, slots // GROUP, group, 0)
    rest = acc[...].reshape(nblk * rows8, block)
    even = odd = None
    spread0, spread1 = half_spread(block, 0), half_spread(block, 1)
    for level in range(3):
        piece = rest.astype(BF16)
        rest = rest - piece.astype(F32)
        e = jnp.dot(piece, spread0, preferred_element_type=F32)
        o = jnp.dot(piece, spread1, preferred_element_type=F32)
        even = e if even is None else even + e
        odd = o if odd is None else odd + o
    even = even.reshape(nblk, rows8, wide)
    odd = odd.reshape(nblk, rows8, wide)
    for b in range(nblk):
        out_ref[:, b * wide:(b + 1) * wide] = even[b, :cases] + odd[b, cases:]


def swap(value, axis, size, mask):
    return lax.ppermute(value, axis, [(i, i ^ mask) for i in range(size)])


def in_hbm(value):
    return pltpu.with_memory_space_constraint(value, pltpu.HBM)


def on_device(velocity, pair_struct, pair_panel, pair_count, mortar_coef, bem_matrix, self_term):
    cases = velocity.shape[0]
    slots, block, _ = mortar_coef.shape
    wide = 2 * block
    node_blocks = velocity.shape[1] // wide
    ncol, nrow = lax.axis_size("col"), lax.axis_size("row")
    rows, width = bem_matrix.shape
    panel_blocks = ncol * width // wide
    half = panel_blocks // (2 * ncol)
    rows8 = 2 * cases
    smem = pl.BlockSpec(memory_space=pltpu.SMEM)
    vmem = pl.BlockSpec(memory_space=pltpu.VMEM)
    hbm = pl.BlockSpec(memory_space=pl.ANY)
    col = lax.axis_index("col")

    keep, send = pl.pallas_call(
        forward_kernel,
        name="mortar_forward",
        out_shape=[jax.ShapeDtypeStruct((ncol, half, rows8, block), F32)] * 2,
        in_specs=[smem] + [hbm] * 4,
        out_specs=[vmem, vmem],
        scratch_shapes=[
            pltpu.VMEM((slots, block, block), BF16),
            pltpu.VMEM(velocity.shape, BF16),
            pltpu.VMEM((node_blocks, rows8, block), F32),
            pltpu.VMEM((panel_blocks, rows8, block), F32),
            pltpu.SMEM(pair_struct.shape, jnp.int32),
            pltpu.SMEM(pair_panel.shape, jnp.int32),
            pltpu.SemaphoreType.DMA((slots // GROUP,)),
            pltpu.SemaphoreType.DMA((3,)),
        ],
        compiler_params=pltpu.CompilerParams(vmem_limit_bytes=16 << 20),
    )(pair_count, *[in_hbm(a) for a in (pair_struct, pair_panel, velocity, mortar_coef)])

    chip = keep + swap(send, "row", nrow, 1)

    def piece(k):
        return lax.dynamic_index_in_dim(chip, col ^ k, 0, keepdims=False)

    plane = piece(0)
    for got in [swap(piece(k).astype(BF16), "col", ncol, k) for k in range(1, ncol)]:
        plane = plane + got.astype(F32)
    sent = plane.astype(BF16)
    whole = plane
    for got in [swap(sent, "row", nrow, 2 * k) for k in range(1, nrow // 2)]:
        whole = whole + got.astype(F32)
    xa = whole.astype(BF16)
    xb = swap(xa, "row", nrow, 1)

    partial_value = pl.pallas_call(
        bem_kernel,
        name="bem_product",
        out_shape=jax.ShapeDtypeStruct((cases, rows), F32),
        in_specs=[vmem, vmem, hbm, hbm],
        out_specs=vmem,
        scratch_shapes=[
            pltpu.VMEM((SLOTS_BEM, min(rows, ROWS_TILE), width), BF16),
            pltpu.VMEM((rows8, width), BF16),
            pltpu.VMEM((rows,), F32),
            pltpu.SemaphoreType.DMA((SLOTS_BEM,)),
            pltpu.SemaphoreType.DMA,
        ],
        compiler_params=pltpu.CompilerParams(vmem_limit_bytes=40 << 20),
    )(xa, xb, in_hbm(self_term), in_hbm(bem_matrix))

    terms = [partial_value] + [swap(partial_value, "col", ncol, k) for k in range(1, ncol)]
    pressure, parts = pl.pallas_call(
        functools.partial(pressure_kernel, ncol),
        name="pressure_sum",
        out_shape=[
            jax.ShapeDtypeStruct((cases, rows), BF16),
            jax.ShapeDtypeStruct((rows // wide, rows8, block), BF16),
        ],
        in_specs=[vmem] * ncol,
        out_specs=[vmem, vmem],
        compiler_params=pltpu.CompilerParams(vmem_limit_bytes=16 << 20),
    )(*terms)

    mine = [parts] + [swap(parts, "row", nrow, 2 * k) for k in range(1, nrow // 2)]
    pieces = []
    for got in mine:
        pieces.append(got)
        pieces.append(swap(got, "row", nrow, 1))

    load = pl.pallas_call(
        functools.partial(backward_kernel, nrow),
        name="mortar_backward",
        out_shape=jax.ShapeDtypeStruct((cases, node_blocks * wide), F32),
        in_specs=[smem, smem, smem, vmem] + [vmem] * nrow,
        out_specs=vmem,
        scratch_shapes=[
            pltpu.VMEM((panel_blocks, rows8, block), F32),
            pltpu.VMEM((node_blocks, rows8, block), F32),
        ],
        compiler_params=pltpu.CompilerParams(vmem_limit_bytes=16 << 20),
    )(pair_struct, pair_panel, pair_count, mortar_coef, *pieces)
    return (pressure, load)


def solution(mesh):
    placed = (
        P(None, ("col", "row")),
        P(("col", "row")),
        P(("col", "row")),
        P(("col", "row")),
        P(("col", "row"), None, None),
        P("row", "col"),
        P("row"),
    )
    return jax.shard_map(
        on_device,
        mesh=mesh,
        in_specs=placed,
        out_specs=(P(None, "row"), P(None, ("col", "row"))),
        check_vma=False,
    )
```

```python
import functools

import jax
import jax.numpy as jnp
from jax import lax
from jax.experimental import pallas as pl
from jax.experimental.pallas import tpu as pltpu
from jax.sharding import PartitionSpec as P


F32 = jnp.float32
BF16 = jnp.bfloat16
GROUP = 16
ROWS_TILE = 256
SLOTS_BEM = 4
HEAD_ROWS = 512


def half_split(block, wide):
    src = lax.broadcasted_iota(jnp.int32, (wide, wide), 0)
    dst = lax.broadcasted_iota(jnp.int32, (wide, wide), 1)
    want = jnp.where(dst < block, 2 * dst, 2 * (dst - block) + 1)
    return jnp.where(src == want, 1.0, 0.0).astype(BF16)


def half_spread(block, part):
    src = lax.broadcasted_iota(jnp.int32, (block, 2 * block), 0)
    dst = lax.broadcasted_iota(jnp.int32, (block, 2 * block), 1)
    return jnp.where(dst == 2 * src + part, 1.0, 0.0).astype(BF16)


def unpack_parts(wide_rows, cases, block):
    nb = wide_rows.shape[0]
    both = jnp.concatenate([wide_rows, wide_rows], axis=1)
    flat = both.reshape(nb * 2 * cases, 2 * block).astype(BF16)
    out = jnp.dot(flat, half_split(block, 2 * block), preferred_element_type=F32)
    out = out.reshape(nb, 2 * cases, 2 * block)
    row = lax.broadcasted_iota(jnp.int32, (nb, 2 * cases, block), 1)
    return jnp.where(row < cases, out[:, :, :block], out[:, :, block:])


def forward_kernel(count_ref, struct_hbm, panel_hbm, vel_hbm, coef_hbm, bem_hbm,
                   keep_ref, send_ref, head_ref, coef,
                   vel_ref, vel, acc, struct_ref, panel_ref,
                   sems, small_sems, head_sem):
    slots, block, _ = coef.shape
    cases = vel_ref.shape[0]
    nblk = vel.shape[0]
    chunks = slots // GROUP
    core = lax.rem(lax.axis_index("row"), 2)

    def fetch(i):
        part = pl.ds(i * GROUP, GROUP)
        return pltpu.make_async_copy(coef_hbm.at[part], coef.at[part], sems.at[i])

    small = [
        pltpu.make_async_copy(src, dst, small_sems.at[n])
        for n, (src, dst) in enumerate(
            [(vel_hbm, vel_ref), (struct_hbm, struct_ref), (panel_hbm, panel_ref)])
    ]
    head_copy = pltpu.make_async_copy(
        bem_hbm.at[pl.ds(0, head_ref.shape[0])], head_ref, head_sem)
    for copy in small:
        copy.start()
    for i in range(chunks):
        fetch(i).start()
    head_copy.start()
    acc[...] = jnp.zeros_like(acc)
    wide = 2 * block
    small[0].wait()
    rows = jnp.stack(
        [vel_ref[:, b * wide:(b + 1) * wide].astype(F32) for b in range(nblk)], axis=0
    )
    vel[...] = unpack_parts(rows, cases, block)
    for copy in small[1:]:
        copy.wait()
    count = count_ref[0]
    zero = jnp.zeros((2 * cases, block), F32)

    def group(i, carry):
        fetch(i).wait()
        base = i * GROUP
        outs = []
        for j in range(0, GROUP, 2):
            qa, qb = base + j, base + j + 1
            va = jnp.where(qa < count, vel[struct_ref[qa]], 0.0)
            vb = jnp.where(qb < count, vel[struct_ref[qb]], 0.0)
            lhs = jnp.concatenate(
                [jnp.concatenate([va, zero], axis=1), jnp.concatenate([zero, vb], axis=1)], axis=0
            ).astype(BF16)
            rhs = jnp.concatenate([coef[qa], coef[qb]], axis=1)
            outs.append(lax.dot_general(lhs, rhs, (((1,), (1,)), ((), ())),
                                        preferred_element_type=F32))
        for j in range(0, GROUP, 2):
            out = outs[j // 2]
            acc[panel_ref[base + j]] += out[:2 * cases]
            acc[panel_ref[base + j + 1]] += out[2 * cases:]
        return carry

    lax.fori_loop(0, chunks, group, 0)
    cols, half = keep_ref.shape[0], keep_ref.shape[1]
    for k in range(cols):
        c = lax.axis_index("col") ^ k
        keep_ref[k] = acc[pl.ds((2 * c + core) * half, half)]
        send_ref[k] = acc[pl.ds((2 * c + 1 - core) * half, half)]
    head_copy.wait()


def bem_kernel(xa_ref, xb_ref, self_hbm, head_ref, bem_hbm, out_ref, tiles, xrow, self_ref, sems, self_sem):
    half, rows8, block = xa_ref.shape
    cases = rows8 // 2
    rows, width = bem_hbm.shape
    tile = tiles.shape[1]
    head = head_ref.shape[0] // tile
    steps = rows // tile - head
    ring = tiles.shape[0]
    row_id = lax.axis_index("row")
    core = lax.rem(row_id, 2)
    wide = 2 * block

    def fetch(i, slot):
        return pltpu.make_async_copy(
            bem_hbm.at[pl.ds((head + i) * tile, tile)], tiles.at[slot], sems.at[slot])

    self_copy = pltpu.make_async_copy(self_hbm, self_ref, self_sem)
    for i in range(min(ring - 1, steps)):
        fetch(i, i).start()
    self_copy.start()
    parts = jnp.concatenate([xa_ref[...], xb_ref[...]], axis=0).astype(F32)
    flat = parts.reshape(2 * half * rows8, block).astype(BF16)
    even = jnp.dot(flat, half_spread(block, 0), preferred_element_type=F32)
    odd = jnp.dot(flat, half_spread(block, 1), preferred_element_type=F32)
    line = lax.broadcasted_iota(jnp.int32, even.shape, 0)
    both = jnp.where(lax.rem(line, rows8) < cases, even, odd)
    both = both.reshape(2 * half, rows8, wide)
    for j in range(half):
        first = jnp.where(core == 0, both[j], both[half + j])
        second = jnp.where(core == 0, both[half + j], both[j])
        xrow[:, j * wide:(j + 1) * wide] = first.astype(BF16)
        xrow[:, (half + j) * wide:(half + j + 1) * wide] = second.astype(BF16)

    def store(i, rows_in):
        got = lax.dot_general(xrow[...], rows_in, (((1,), (1,)), ((), ())),
                              preferred_element_type=F32)
        out_ref[:, pl.ds(pl.multiple_of(i * tile, tile), tile)] = got[:cases] + got[cases:]

    def head_step(i, carry):
        store(i, head_ref[pl.ds(pl.multiple_of(i * tile, tile), tile)])
        return carry

    lax.fori_loop(0, head, head_step, 0)

    def step(i, carry):
        slot = lax.rem(i, ring)
        fetch(i, slot).wait()

        @pl.when(i + ring - 1 < steps)
        def _():
            fetch(i + ring - 1, lax.rem(i + ring - 1, ring)).start()

        store(head + i, tiles[slot])
        return carry

    lax.fori_loop(0, steps, step, 0)
    start = row_id * rows
    self_copy.wait()

    @pl.when(start // width == lax.axis_index("col"))
    def _():
        offset = pl.multiple_of(lax.rem(start, width), rows)
        own = xrow[:, pl.ds(offset, rows)].astype(F32)
        out_ref[...] += self_ref[...][None, :] * (own[:cases] + own[cases:])


def backward_kernel(ranks, struct_hbm, panel_hbm, count_ref, coef, *refs):
    pieces, scratch = refs[:ranks], refs[ranks:]
    out_ref, table, acc, struct_ref, panel_ref, sems = scratch
    small = [
        pltpu.make_async_copy(src, dst, sems.at[n])
        for n, (src, dst) in enumerate(
            [(struct_hbm, struct_ref), (panel_hbm, panel_ref)])
    ]
    for copy in small:
        copy.start()
    slots, block, _ = coef.shape
    nblk, rows8, _ = acc.shape
    cases = rows8 // 2
    wide = 2 * block
    me = lax.axis_index("row")
    per = pieces[0].shape[1] // wide
    for k in range(ranks):
        rows = jnp.stack(
            [pieces[k][:, b * wide:(b + 1) * wide].astype(F32) for b in range(per)], axis=0)
        table[pl.ds((me ^ k) * per, per)] = unpack_parts(rows, cases, block)
    acc[...] = jnp.zeros_like(acc)
    for copy in small:
        copy.wait()
    count = count_ref[0]

    def group(i, carry):
        base = i * GROUP
        outs = []
        for j in range(0, GROUP, 2):
            qa, qb = base + j, base + j + 1
            pa = jnp.where(qa < count, table[panel_ref[qa]], 0.0)
            pb = jnp.where(qb < count, table[panel_ref[qb]], 0.0)
            lhs = jnp.concatenate([pa, pb], axis=0).astype(BF16)
            rhs = jnp.concatenate([coef[qa], coef[qb]], axis=1)
            outs.append(jnp.dot(lhs, rhs, preferred_element_type=F32))
        for j in range(0, GROUP, 2):
            out = outs[j // 2]
            acc[struct_ref[base + j]] += out[:rows8, :block]
            acc[struct_ref[base + j + 1]] += out[rows8:, block:]
        return carry

    lax.fori_loop(0, slots // GROUP, group, 0)
    rest = acc[...].reshape(nblk * rows8, block)
    even = odd = None
    spread0, spread1 = half_spread(block, 0), half_spread(block, 1)
    for level in range(3):
        piece = rest.astype(BF16)
        rest = rest - piece.astype(F32)
        e = jnp.dot(piece, spread0, preferred_element_type=F32)
        o = jnp.dot(piece, spread1, preferred_element_type=F32)
        even = e if even is None else even + e
        odd = o if odd is None else odd + o
    even = even.reshape(nblk, rows8, wide)
    odd = odd.reshape(nblk, rows8, wide)
    for b in range(nblk):
        out_ref[:, b * wide:(b + 1) * wide] = even[b, :cases] + odd[b, cases:]


def swap(value, axis, size, mask):
    return lax.ppermute(value, axis, [(i, i ^ mask) for i in range(size)])


def in_hbm(value):
    return pltpu.with_memory_space_constraint(value, pltpu.HBM)


def on_device(velocity, pair_struct, pair_panel, pair_count, mortar_coef, bem_matrix, self_term):
    cases = velocity.shape[0]
    slots, block, _ = mortar_coef.shape
    wide = 2 * block
    node_blocks = velocity.shape[1] // wide
    ncol, nrow = lax.axis_size("col"), lax.axis_size("row")
    rows, width = bem_matrix.shape
    panel_blocks = ncol * width // wide
    half = panel_blocks // (2 * ncol)
    rows8 = 2 * cases
    smem = pl.BlockSpec(memory_space=pltpu.SMEM)
    vmem = pl.BlockSpec(memory_space=pltpu.VMEM)
    hbm = pl.BlockSpec(memory_space=pl.ANY)

    head_rows = min(HEAD_ROWS, rows // 2)
    keep, send, head, coef = pl.pallas_call(
        forward_kernel,
        name="mortar_forward",
        out_shape=[
            jax.ShapeDtypeStruct((ncol, half, rows8, block), F32),
            jax.ShapeDtypeStruct((ncol, half, rows8, block), F32),
            pltpu.VMEM((head_rows, width), BF16),
            pltpu.VMEM(mortar_coef.shape, BF16),
        ],
        in_specs=[smem] + [hbm] * 5,
        out_specs=[vmem] * 4,
        scratch_shapes=[
            pltpu.VMEM(velocity.shape, BF16),
            pltpu.VMEM((node_blocks, rows8, block), F32),
            pltpu.VMEM((panel_blocks, rows8, block), F32),
            pltpu.SMEM(pair_struct.shape, jnp.int32),
            pltpu.SMEM(pair_panel.shape, jnp.int32),
            pltpu.SemaphoreType.DMA((slots // GROUP,)),
            pltpu.SemaphoreType.DMA((3,)),
            pltpu.SemaphoreType.DMA,
        ],
        compiler_params=pltpu.CompilerParams(vmem_limit_bytes=16 << 20),
    )(pair_count, *[in_hbm(a) for a in
                    (pair_struct, pair_panel, velocity, mortar_coef, bem_matrix)])

    chip = keep + swap(send, "row", nrow, 1)
    plane = chip[0]
    for got in [swap(chip[k], "col", ncol, k) for k in range(1, ncol)]:
        plane = plane + got
    sent = plane.astype(BF16)
    whole = plane
    for got in [swap(sent, "row", nrow, 2 * k) for k in range(1, nrow // 2)]:
        whole = whole + got.astype(F32)
    xa = whole.astype(BF16)
    xb = swap(xa, "row", nrow, 1)

    partial_value = pl.pallas_call(
        bem_kernel,
        name="bem_product",
        out_shape=jax.ShapeDtypeStruct((cases, rows), F32),
        in_specs=[vmem, vmem, hbm, vmem, hbm],
        out_specs=vmem,
        scratch_shapes=[
            pltpu.VMEM((SLOTS_BEM, min(head_rows, ROWS_TILE), width), BF16),
            pltpu.VMEM((rows8, width), BF16),
            pltpu.VMEM((rows,), F32),
            pltpu.SemaphoreType.DMA((SLOTS_BEM,)),
            pltpu.SemaphoreType.DMA,
        ],
        compiler_params=pltpu.CompilerParams(vmem_limit_bytes=24 << 20),
    )(xa, xb, in_hbm(self_term), pltpu.with_memory_space_constraint(head, pltpu.VMEM),
      in_hbm(bem_matrix))

    total = partial_value
    for got in [swap(partial_value, "col", ncol, k) for k in range(1, ncol)]:
        total = total + got
    pressure = total.astype(BF16)

    mine = [pressure] + [swap(pressure, "row", nrow, 2 * k) for k in range(1, nrow // 2)]
    pieces = []
    for got in mine:
        pieces.append(got)
        pieces.append(swap(got, "row", nrow, 1))

    load = pl.pallas_call(
        functools.partial(backward_kernel, nrow),
        name="mortar_backward",
        out_shape=jax.ShapeDtypeStruct((cases, node_blocks * wide), F32),
        in_specs=[hbm, hbm, smem, vmem] + [vmem] * nrow,
        out_specs=vmem,
        scratch_shapes=[
            pltpu.VMEM((panel_blocks, rows8, block), F32),
            pltpu.VMEM((node_blocks, rows8, block), F32),
            pltpu.SMEM(pair_struct.shape, jnp.int32),
            pltpu.SMEM(pair_panel.shape, jnp.int32),
            pltpu.SemaphoreType.DMA((2,)),
        ],
        compiler_params=pltpu.CompilerParams(vmem_limit_bytes=16 << 20),
    )(in_hbm(pair_struct), in_hbm(pair_panel), pair_count, coef, *pieces)
    return (pressure, load)


def solution(mesh):
    placed = (
        P(None, ("col", "row")),
        P(("col", "row")),
        P(("col", "row")),
        P(("col", "row")),
        P(("col", "row"), None, None),
        P("row", "col"),
        P("row"),
    )
    return jax.shard_map(
        on_device,
        mesh=mesh,
        in_specs=placed,
        out_specs=(P(None, "row"), P(None, ("col", "row"))),
        check_vma=False,
    )
```

```python
import functools

import jax
import jax.numpy as jnp
from jax import lax
from jax.experimental import pallas as pl
from jax.experimental.pallas import tpu as pltpu
from jax.sharding import PartitionSpec as P


F32 = jnp.float32
BF16 = jnp.bfloat16
FORWARD_GROUP = 32
BACKWARD_GROUP = 64
ROWS_TILE = 512
SLOTS_BEM = 3
HEAD_ROWS = 512


def half_split(block, wide):
    src = lax.broadcasted_iota(jnp.int32, (wide, wide), 0)
    dst = lax.broadcasted_iota(jnp.int32, (wide, wide), 1)
    want = jnp.where(dst < block, 2 * dst, 2 * (dst - block) + 1)
    return jnp.where(src == want, 1.0, 0.0).astype(BF16)


def half_spread(block, part):
    src = lax.broadcasted_iota(jnp.int32, (block, 2 * block), 0)
    dst = lax.broadcasted_iota(jnp.int32, (block, 2 * block), 1)
    return jnp.where(dst == 2 * src + part, 1.0, 0.0).astype(BF16)


def unpack_parts(wide_rows, cases, block):
    nb = wide_rows.shape[0]
    both = jnp.concatenate([wide_rows, wide_rows], axis=1)
    flat = both.reshape(nb * 2 * cases, 2 * block).astype(BF16)
    out = jnp.dot(flat, half_split(block, 2 * block), preferred_element_type=F32)
    out = out.reshape(nb, 2 * cases, 2 * block)
    row = lax.broadcasted_iota(jnp.int32, (nb, 2 * cases, block), 1)
    return jnp.where(row < cases, out[:, :, :block], out[:, :, block:])


def forward_kernel(count_ref, struct_hbm, panel_hbm, vel_hbm, coef_hbm, bem_hbm,
                   keep_ref, send_ref, head_ref, coef,
                   vel_ref, vel, acc, struct_ref, panel_ref,
                   sems, small_sems, head_sem):
    slots, block, _ = coef.shape
    cases = vel_ref.shape[0]
    nblk = vel.shape[0]
    chunks = slots // FORWARD_GROUP
    core = lax.rem(lax.axis_index("row"), 2)

    def fetch(i):
        part = pl.ds(i * FORWARD_GROUP, FORWARD_GROUP)
        return pltpu.make_async_copy(coef_hbm.at[part], coef.at[part], sems.at[i])

    small = [
        pltpu.make_async_copy(src, dst, small_sems.at[n])
        for n, (src, dst) in enumerate(
            [(vel_hbm, vel_ref), (struct_hbm, struct_ref), (panel_hbm, panel_ref)])
    ]
    head_copy = pltpu.make_async_copy(
        bem_hbm.at[pl.ds(0, head_ref.shape[0])], head_ref, head_sem)
    for copy in small:
        copy.start()
    for i in range(chunks):
        fetch(i).start()
    head_copy.start()
    acc[...] = jnp.zeros_like(acc)
    wide = 2 * block
    small[0].wait()
    rows = jnp.stack(
        [vel_ref[:, b * wide:(b + 1) * wide].astype(F32) for b in range(nblk)], axis=0
    )
    vel[...] = unpack_parts(rows, cases, block)
    for copy in small[1:]:
        copy.wait()
    count = count_ref[0]
    zero = jnp.zeros((2 * cases, block), F32)

    def group(i, carry):
        fetch(i).wait()
        base = i * FORWARD_GROUP
        outs = []
        for j in range(0, FORWARD_GROUP, 2):
            qa, qb = base + j, base + j + 1
            va = jnp.where(qa < count, vel[struct_ref[qa]], 0.0)
            vb = jnp.where(qb < count, vel[struct_ref[qb]], 0.0)
            lhs = jnp.concatenate(
                [jnp.concatenate([va, zero], axis=1), jnp.concatenate([zero, vb], axis=1)], axis=0
            ).astype(BF16)
            rhs = jnp.concatenate([coef[qa], coef[qb]], axis=1)
            outs.append(lax.dot_general(lhs, rhs, (((1,), (1,)), ((), ())),
                                        preferred_element_type=F32))
        for j in range(0, FORWARD_GROUP, 2):
            out = outs[j // 2]
            acc[panel_ref[base + j]] += out[:2 * cases]
            acc[panel_ref[base + j + 1]] += out[2 * cases:]
        return carry

    lax.fori_loop(0, chunks, group, 0)
    cols, half = keep_ref.shape[0], keep_ref.shape[1]
    for k in range(cols):
        c = lax.axis_index("col") ^ k
        keep_ref[k] = acc[pl.ds((2 * c + core) * half, half)]
        send_ref[k] = acc[pl.ds((2 * c + 1 - core) * half, half)]
    head_copy.wait()


def bem_kernel(xa_ref, xb_ref, self_hbm, head_ref, bem_hbm, out_ref, tiles, xrow, self_ref, sems, self_sem):
    half, rows8, block = xa_ref.shape
    cases = rows8 // 2
    rows, width = bem_hbm.shape
    tile = tiles.shape[1]
    head = head_ref.shape[0] // tile
    steps = rows // tile - head
    ring = tiles.shape[0]
    row_id = lax.axis_index("row")
    core = lax.rem(row_id, 2)
    wide = 2 * block

    def fetch(i, slot):
        return pltpu.make_async_copy(
            bem_hbm.at[pl.ds((head + i) * tile, tile)], tiles.at[slot], sems.at[slot])

    self_copy = pltpu.make_async_copy(self_hbm, self_ref, self_sem)
    for i in range(min(ring - 1, steps)):
        fetch(i, i).start()
    self_copy.start()
    parts = jnp.concatenate([xa_ref[...], xb_ref[...]], axis=0).astype(F32)
    flat = parts.reshape(2 * half * rows8, block).astype(BF16)
    even = jnp.dot(flat, half_spread(block, 0), preferred_element_type=F32)
    odd = jnp.dot(flat, half_spread(block, 1), preferred_element_type=F32)
    line = lax.broadcasted_iota(jnp.int32, even.shape, 0)
    both = jnp.where(lax.rem(line, rows8) < cases, even, odd)
    both = both.reshape(2 * half, rows8, wide)
    for j in range(half):
        first = jnp.where(core == 0, both[j], both[half + j])
        second = jnp.where(core == 0, both[half + j], both[j])
        xrow[:, j * wide:(j + 1) * wide] = first.astype(BF16)
        xrow[:, (half + j) * wide:(half + j + 1) * wide] = second.astype(BF16)

    def store(i, rows_in):
        got = lax.dot_general(xrow[...], rows_in, (((1,), (1,)), ((), ())),
                              preferred_element_type=F32)
        out_ref[:, pl.ds(pl.multiple_of(i * tile, tile), tile)] = got[:cases] + got[cases:]

    def head_step(i, carry):
        store(i, head_ref[pl.ds(pl.multiple_of(i * tile, tile), tile)])
        return carry

    lax.fori_loop(0, head, head_step, 0)

    def step(i, carry):
        slot = lax.rem(i, ring)
        fetch(i, slot).wait()

        @pl.when(i + ring - 1 < steps)
        def _():
            fetch(i + ring - 1, lax.rem(i + ring - 1, ring)).start()

        store(head + i, tiles[slot])
        return carry

    lax.fori_loop(0, steps, step, 0)
    start = row_id * rows
    self_copy.wait()

    @pl.when(start // width == lax.axis_index("col"))
    def _():
        offset = pl.multiple_of(lax.rem(start, width), rows)
        own = xrow[:, pl.ds(offset, rows)].astype(F32)
        out_ref[...] += self_ref[...][None, :] * (own[:cases] + own[cases:])


def backward_kernel(ranks, struct_hbm, panel_hbm, count_ref, coef, *refs):
    pieces, scratch = refs[:ranks], refs[ranks:]
    out_ref, table, acc, struct_ref, panel_ref, sems = scratch
    small = [
        pltpu.make_async_copy(src, dst, sems.at[n])
        for n, (src, dst) in enumerate(
            [(struct_hbm, struct_ref), (panel_hbm, panel_ref)])
    ]
    for copy in small:
        copy.start()
    slots, block, _ = coef.shape
    nblk, rows8, _ = acc.shape
    cases = rows8 // 2
    wide = 2 * block
    me = lax.axis_index("row")
    per = pieces[0].shape[1] // wide
    for k in range(ranks):
        rows = jnp.stack(
            [pieces[k][:, b * wide:(b + 1) * wide].astype(F32) for b in range(per)], axis=0)
        table[pl.ds((me ^ k) * per, per)] = unpack_parts(rows, cases, block)
    acc[...] = jnp.zeros_like(acc)
    for copy in small:
        copy.wait()
    count = count_ref[0]

    def group(i, carry):
        base = i * BACKWARD_GROUP
        outs = []
        for j in range(0, BACKWARD_GROUP, 2):
            qa, qb = base + j, base + j + 1
            pa = jnp.where(qa < count, table[panel_ref[qa]], 0.0)
            pb = jnp.where(qb < count, table[panel_ref[qb]], 0.0)
            lhs = jnp.concatenate([pa, pb], axis=0).astype(BF16)
            rhs = jnp.concatenate([coef[qa], coef[qb]], axis=1)
            outs.append(jnp.dot(lhs, rhs, preferred_element_type=F32))
        for j in range(0, BACKWARD_GROUP, 2):
            out = outs[j // 2]
            acc[struct_ref[base + j]] += out[:rows8, :block]
            acc[struct_ref[base + j + 1]] += out[rows8:, block:]
        return carry

    lax.fori_loop(0, slots // BACKWARD_GROUP, group, 0)
    rest = acc[...].reshape(nblk * rows8, block)
    even = odd = None
    spread0, spread1 = half_spread(block, 0), half_spread(block, 1)
    for level in range(3):
        piece = rest.astype(BF16)
        rest = rest - piece.astype(F32)
        e = jnp.dot(piece, spread0, preferred_element_type=F32)
        o = jnp.dot(piece, spread1, preferred_element_type=F32)
        even = e if even is None else even + e
        odd = o if odd is None else odd + o
    even = even.reshape(nblk, rows8, wide)
    odd = odd.reshape(nblk, rows8, wide)
    for b in range(nblk):
        out_ref[:, b * wide:(b + 1) * wide] = even[b, :cases] + odd[b, cases:]


def swap(value, axis, size, mask):
    return lax.ppermute(value, axis, [(i, i ^ mask) for i in range(size)])


def in_hbm(value):
    return pltpu.with_memory_space_constraint(value, pltpu.HBM)


def on_device(velocity, pair_struct, pair_panel, pair_count, mortar_coef, bem_matrix, self_term):
    cases = velocity.shape[0]
    slots, block, _ = mortar_coef.shape
    wide = 2 * block
    node_blocks = velocity.shape[1] // wide
    ncol, nrow = lax.axis_size("col"), lax.axis_size("row")
    rows, width = bem_matrix.shape
    panel_blocks = ncol * width // wide
    half = panel_blocks // (2 * ncol)
    rows8 = 2 * cases
    smem = pl.BlockSpec(memory_space=pltpu.SMEM)
    vmem = pl.BlockSpec(memory_space=pltpu.VMEM)
    hbm = pl.BlockSpec(memory_space=pl.ANY)

    head_rows = min(HEAD_ROWS, rows // 2)
    keep, send, head, coef = pl.pallas_call(
        forward_kernel,
        name="mortar_forward",
        out_shape=[
            jax.ShapeDtypeStruct((ncol, half, rows8, block), F32),
            jax.ShapeDtypeStruct((ncol, half, rows8, block), F32),
            pltpu.VMEM((head_rows, width), BF16),
            pltpu.VMEM(mortar_coef.shape, BF16),
        ],
        in_specs=[smem] + [hbm] * 5,
        out_specs=[vmem] * 4,
        scratch_shapes=[
            pltpu.VMEM(velocity.shape, BF16),
            pltpu.VMEM((node_blocks, rows8, block), F32),
            pltpu.VMEM((panel_blocks, rows8, block), F32),
            pltpu.SMEM(pair_struct.shape, jnp.int32),
            pltpu.SMEM(pair_panel.shape, jnp.int32),
            pltpu.SemaphoreType.DMA((slots // FORWARD_GROUP,)),
            pltpu.SemaphoreType.DMA((3,)),
            pltpu.SemaphoreType.DMA,
        ],
        compiler_params=pltpu.CompilerParams(vmem_limit_bytes=16 << 20),
    )(pair_count, *[in_hbm(a) for a in
                    (pair_struct, pair_panel, velocity, mortar_coef, bem_matrix)])

    chip = keep + swap(send, "row", nrow, 1)
    plane = chip[0]
    for got in [swap(chip[k], "col", ncol, k) for k in range(1, ncol)]:
        plane = plane + got
    sent = plane.astype(BF16)
    whole = plane
    for got in [swap(sent, "row", nrow, 2 * k) for k in range(1, nrow // 2)]:
        whole = whole + got.astype(F32)
    xa = whole.astype(BF16)
    xb = swap(xa, "row", nrow, 1)

    partial_value = pl.pallas_call(
        bem_kernel,
        name="bem_product",
        out_shape=jax.ShapeDtypeStruct((cases, rows), F32),
        in_specs=[vmem, vmem, hbm, vmem, hbm],
        out_specs=vmem,
        scratch_shapes=[
            pltpu.VMEM((SLOTS_BEM, min(head_rows, ROWS_TILE), width), BF16),
            pltpu.VMEM((rows8, width), BF16),
            pltpu.VMEM((rows,), F32),
            pltpu.SemaphoreType.DMA((SLOTS_BEM,)),
            pltpu.SemaphoreType.DMA,
        ],
        compiler_params=pltpu.CompilerParams(vmem_limit_bytes=32 << 20),
    )(xa, xb, in_hbm(self_term), pltpu.with_memory_space_constraint(head, pltpu.VMEM),
      in_hbm(bem_matrix))

    total = partial_value
    for got in [swap(partial_value, "col", ncol, k) for k in range(1, ncol)]:
        total = total + got
    pressure = total.astype(BF16)

    mine = [pressure] + [swap(pressure, "row", nrow, 2 * k) for k in range(1, nrow // 2)]
    pieces = []
    for got in mine:
        pieces.append(got)
        pieces.append(swap(got, "row", nrow, 1))

    load = pl.pallas_call(
        functools.partial(backward_kernel, nrow),
        name="mortar_backward",
        out_shape=jax.ShapeDtypeStruct((cases, node_blocks * wide), F32),
        in_specs=[hbm, hbm, smem, vmem] + [vmem] * nrow,
        out_specs=vmem,
        scratch_shapes=[
            pltpu.VMEM((panel_blocks, rows8, block), F32),
            pltpu.VMEM((node_blocks, rows8, block), F32),
            pltpu.SMEM(pair_struct.shape, jnp.int32),
            pltpu.SMEM(pair_panel.shape, jnp.int32),
            pltpu.SemaphoreType.DMA((2,)),
        ],
        compiler_params=pltpu.CompilerParams(vmem_limit_bytes=16 << 20),
    )(in_hbm(pair_struct), in_hbm(pair_panel), pair_count, coef, *pieces)
    return (pressure, load)


def solution(mesh):
    placed = (
        P(None, ("col", "row")),
        P(("col", "row")),
        P(("col", "row")),
        P(("col", "row")),
        P(("col", "row"), None, None),
        P("row", "col"),
        P("row"),
    )
    return jax.shard_map(
        on_device,
        mesh=mesh,
        in_specs=placed,
        out_specs=(P(None, "row"), P(None, ("col", "row"))),
        check_vma=False,
    )
```

```python
import functools

import jax
import jax.numpy as jnp
from jax import lax
from jax.experimental import pallas as pl
from jax.experimental.pallas import tpu as pltpu
from jax.sharding import PartitionSpec as P


F32 = jnp.float32
BF16 = jnp.bfloat16
FORWARD_GROUP = 32
BACKWARD_GROUP = 64
HEAD_ROWS = 256
WINDOW_ROWS = 256
CHUNK_ROWS = 256
BODY_CHUNKS = 2
BUFFER_ROWS = 1536


def half_split(block, wide):
    src = lax.broadcasted_iota(jnp.int32, (wide, wide), 0)
    dst = lax.broadcasted_iota(jnp.int32, (wide, wide), 1)
    want = jnp.where(dst < block, 2 * dst, 2 * (dst - block) + 1)
    return jnp.where(src == want, 1.0, 0.0).astype(BF16)


def half_spread(block, part):
    src = lax.broadcasted_iota(jnp.int32, (block, 2 * block), 0)
    dst = lax.broadcasted_iota(jnp.int32, (block, 2 * block), 1)
    return jnp.where(dst == 2 * src + part, 1.0, 0.0).astype(BF16)


def unpack_parts(wide_rows, cases, block):
    nb = wide_rows.shape[0]
    both = jnp.concatenate([wide_rows, wide_rows], axis=1)
    flat = both.reshape(nb * 2 * cases, 2 * block).astype(BF16)
    out = jnp.dot(flat, half_split(block, 2 * block), preferred_element_type=F32)
    out = out.reshape(nb, 2 * cases, 2 * block)
    row = lax.broadcasted_iota(jnp.int32, (nb, 2 * cases, block), 1)
    return jnp.where(row < cases, out[:, :, :block], out[:, :, block:])


def forward_kernel(head_rows, count_ref, struct_hbm, panel_hbm, vel_hbm, coef_hbm, bem_hbm,
                   keep_ref, send_ref, head_ref, coef,
                   vel_ref, vel, acc, struct_ref, panel_ref,
                   sems, small_sems, head_sem):
    slots, block, _ = coef.shape
    cases = vel_ref.shape[0]
    nblk = vel.shape[0]
    chunks = slots // FORWARD_GROUP
    core = lax.rem(lax.axis_index("row"), 2)

    def fetch(i):
        part = pl.ds(i * FORWARD_GROUP, FORWARD_GROUP)
        return pltpu.make_async_copy(coef_hbm.at[part], coef.at[part], sems.at[i])

    small = [
        pltpu.make_async_copy(src, dst, small_sems.at[n])
        for n, (src, dst) in enumerate(
            [(vel_hbm, vel_ref), (struct_hbm, struct_ref), (panel_hbm, panel_ref)])
    ]
    head_copy = pltpu.make_async_copy(
        bem_hbm.at[pl.ds(0, head_rows)], head_ref.at[pl.ds(0, head_rows)], head_sem)
    for copy in small:
        copy.start()
    for i in range(chunks):
        fetch(i).start()
    head_copy.start()
    acc[...] = jnp.zeros_like(acc)
    wide = 2 * block
    small[0].wait()
    rows = jnp.stack(
        [vel_ref[:, b * wide:(b + 1) * wide].astype(F32) for b in range(nblk)], axis=0
    )
    vel[...] = unpack_parts(rows, cases, block)
    for copy in small[1:]:
        copy.wait()
    count = count_ref[0]
    zero = jnp.zeros((2 * cases, block), F32)

    def group(i, carry):
        fetch(i).wait()
        base = i * FORWARD_GROUP
        outs = []
        for j in range(0, FORWARD_GROUP, 2):
            qa, qb = base + j, base + j + 1
            va = jnp.where(qa < count, vel[struct_ref[qa]], 0.0)
            vb = jnp.where(qb < count, vel[struct_ref[qb]], 0.0)
            lhs = jnp.concatenate(
                [jnp.concatenate([va, zero], axis=1), jnp.concatenate([zero, vb], axis=1)], axis=0
            ).astype(BF16)
            rhs = jnp.concatenate([coef[qa], coef[qb]], axis=1)
            outs.append(lax.dot_general(lhs, rhs, (((1,), (1,)), ((), ())),
                                        preferred_element_type=F32))
        for j in range(0, FORWARD_GROUP, 2):
            out = outs[j // 2]
            acc[panel_ref[base + j]] += out[:2 * cases]
            acc[panel_ref[base + j + 1]] += out[2 * cases:]
        return carry

    lax.fori_loop(0, chunks, group, 0)
    cols, half = keep_ref.shape[0], keep_ref.shape[1]
    for k in range(cols):
        c = lax.axis_index("col") ^ k
        keep_ref[k] = acc[pl.ds((2 * c + core) * half, half)]
        send_ref[k] = acc[pl.ds((2 * c + 1 - core) * half, half)]
    head_copy.wait()


def fetch_kernel(start, count, after_ref, held_ref, bem_hbm, out_ref, sem):
    part = pl.ds(start, count)
    copy = pltpu.make_async_copy(bem_hbm.at[part], out_ref.at[part], sem)
    copy.start()
    copy.wait()


def fetch_rows(start, count, after, held, bem_matrix):
    hbm = pl.BlockSpec(memory_space=pl.ANY)
    vmem = pl.BlockSpec(memory_space=pltpu.VMEM)
    return pl.pallas_call(
        functools.partial(fetch_kernel, start, count),
        name="fetch_rows",
        out_shape=pltpu.VMEM(held.shape, BF16),
        in_specs=[hbm, vmem, hbm],
        out_specs=vmem,
        scratch_shapes=[pltpu.SemaphoreType.DMA],
        input_output_aliases={1: 0},
        compiler_params=pltpu.CompilerParams(vmem_limit_bytes=1 << 20),
        cost_estimate=pl.CostEstimate(
            flops=0, transcendentals=0, bytes_accessed=2 * count * held.shape[1]),
    )(after, held, in_hbm(bem_matrix))


def bem_kernel(ready, per, xa_ref, xb_ref, self_hbm, held_ref, bem_hbm, out_ref, tiles,
               xrow, self_ref, sems, self_sem):
    half, rows8, block = xa_ref.shape
    cases = rows8 // 2
    rows, width = bem_hbm.shape
    ring = sems.shape[0]
    chunk = tiles.shape[0] // ring
    chunks = rows // chunk
    tile = per * chunk
    row_id = lax.axis_index("row")
    core = lax.rem(row_id, 2)
    wide = 2 * block

    def fetch(i):
        slot = lax.rem(i, ring)
        to = pl.ds(pl.multiple_of(slot * chunk, chunk), chunk)
        return pltpu.make_async_copy(
            bem_hbm.at[pl.ds(pl.multiple_of(i * chunk, chunk), chunk)], tiles.at[to],
            sems.at[slot])

    self_copy = pltpu.make_async_copy(self_hbm, self_ref, self_sem)
    for i in range(ready, min(ready + 1, ring, chunks)):
        fetch(i).start()
    parts = jnp.concatenate([xa_ref[...], xb_ref[...]], axis=0).astype(F32)
    flat = parts.reshape(2 * half * rows8, block).astype(BF16)
    even = jnp.dot(flat, half_spread(block, 0), preferred_element_type=F32)
    odd = jnp.dot(flat, half_spread(block, 1), preferred_element_type=F32)
    line = lax.broadcasted_iota(jnp.int32, even.shape, 0)
    both = jnp.where(lax.rem(line, rows8) < cases, even, odd)
    both = both.reshape(2 * half, rows8, wide)
    for j in range(half):
        first = jnp.where(core == 0, both[j], both[half + j])
        second = jnp.where(core == 0, both[half + j], both[j])
        xrow[:, j * wide:(j + 1) * wide] = first.astype(BF16)
        xrow[:, (half + j) * wide:(half + j + 1) * wide] = second.astype(BF16)

    for i in range(ready + 1, min(ring, chunks)):
        fetch(i).start()
    self_copy.start()

    def step(i, carry):
        for n in range(per):
            @pl.when(i * per + n >= ready)
            def _(n=n):
                fetch(i * per + n).wait()

            @pl.when(jnp.logical_and(i >= 1, (i - 1) * per + n + ring < chunks))
            def _(n=n):
                fetch((i - 1) * per + n + ring).start()

        slot = lax.rem(i, ring // per)
        got = lax.dot_general(
            xrow[...], tiles[pl.ds(pl.multiple_of(slot * tile, tile), tile)],
            (((1,), (1,)), ((), ())), preferred_element_type=F32)
        out_ref[:, pl.ds(pl.multiple_of(i * tile, tile), tile)] = got[:cases] + got[cases:]
        return carry

    lax.fori_loop(0, chunks // per, step, 0)
    start = row_id * rows
    self_copy.wait()

    @pl.when(start // width == lax.axis_index("col"))
    def _():
        offset = pl.multiple_of(lax.rem(start, width), rows)
        own = xrow[:, pl.ds(offset, rows)].astype(F32)
        out_ref[...] += self_ref[...][None, :] * (own[:cases] + own[cases:])


def backward_kernel(ranks, struct_hbm, panel_hbm, count_ref, coef, *refs):
    pieces, scratch = refs[:ranks], refs[ranks:]
    out_ref, table, acc, struct_ref, panel_ref, sems = scratch
    small = [
        pltpu.make_async_copy(src, dst, sems.at[n])
        for n, (src, dst) in enumerate(
            [(struct_hbm, struct_ref), (panel_hbm, panel_ref)])
    ]
    for copy in small:
        copy.start()
    slots, block, _ = coef.shape
    nblk, rows8, _ = acc.shape
    cases = rows8 // 2
    wide = 2 * block
    me = lax.axis_index("row")
    per = pieces[0].shape[1] // wide
    for k in range(ranks):
        rows = jnp.stack(
            [pieces[k][:, b * wide:(b + 1) * wide].astype(F32) for b in range(per)], axis=0)
        table[pl.ds((me ^ k) * per, per)] = unpack_parts(rows, cases, block)
    acc[...] = jnp.zeros_like(acc)
    for copy in small:
        copy.wait()
    count = count_ref[0]

    def group(i, carry):
        base = i * BACKWARD_GROUP
        outs = []
        for j in range(0, BACKWARD_GROUP, 2):
            qa, qb = base + j, base + j + 1
            pa = jnp.where(qa < count, table[panel_ref[qa]], 0.0)
            pb = jnp.where(qb < count, table[panel_ref[qb]], 0.0)
            lhs = jnp.concatenate([pa, pb], axis=0).astype(BF16)
            rhs = jnp.concatenate([coef[qa], coef[qb]], axis=1)
            outs.append(jnp.dot(lhs, rhs, preferred_element_type=F32))
        for j in range(0, BACKWARD_GROUP, 2):
            out = outs[j // 2]
            acc[struct_ref[base + j]] += out[:rows8, :block]
            acc[struct_ref[base + j + 1]] += out[rows8:, block:]
        return carry

    lax.fori_loop(0, slots // BACKWARD_GROUP, group, 0)
    rest = acc[...].reshape(nblk * rows8, block)
    even = odd = None
    spread0, spread1 = half_spread(block, 0), half_spread(block, 1)
    for _ in range(3):
        piece = rest.astype(BF16)
        rest = rest - piece.astype(F32)
        e = jnp.dot(piece, spread0, preferred_element_type=F32)
        o = jnp.dot(piece, spread1, preferred_element_type=F32)
        even = e if even is None else even + e
        odd = o if odd is None else odd + o
    even = even.reshape(nblk, rows8, wide)
    odd = odd.reshape(nblk, rows8, wide)
    for b in range(nblk):
        out_ref[:, b * wide:(b + 1) * wide] = even[b, :cases] + odd[b, cases:]


def swap(value, axis, size, mask):
    return lax.ppermute(value, axis, [(i, i ^ mask) for i in range(size)])


def in_hbm(value):
    return pltpu.with_memory_space_constraint(value, pltpu.HBM)


def on_device(velocity, pair_struct, pair_panel, pair_count, mortar_coef, bem_matrix, self_term):
    cases = velocity.shape[0]
    slots, block, _ = mortar_coef.shape
    wide = 2 * block
    node_blocks = velocity.shape[1] // wide
    ncol, nrow = lax.axis_size("col"), lax.axis_size("row")
    rows, width = bem_matrix.shape
    panel_blocks = ncol * width // wide
    half = panel_blocks // (2 * ncol)
    rows8 = 2 * cases
    smem = pl.BlockSpec(memory_space=pltpu.SMEM)
    vmem = pl.BlockSpec(memory_space=pltpu.VMEM)
    hbm = pl.BlockSpec(memory_space=pl.ANY)

    head_rows = min(HEAD_ROWS, rows // 4)
    window_rows = min(WINDOW_ROWS, rows // 4)
    chunk_rows = min(CHUNK_ROWS, rows // 4)
    buffer_rows = min(BUFFER_ROWS, rows)
    keep, send, held, coef = pl.pallas_call(
        functools.partial(forward_kernel, head_rows),
        name="mortar_forward",
        out_shape=[
            jax.ShapeDtypeStruct((ncol, half, rows8, block), F32),
            jax.ShapeDtypeStruct((ncol, half, rows8, block), F32),
            pltpu.VMEM((buffer_rows, width), BF16),
            pltpu.VMEM(mortar_coef.shape, BF16),
        ],
        in_specs=[smem] + [hbm] * 5,
        out_specs=[vmem] * 4,
        scratch_shapes=[
            pltpu.VMEM(velocity.shape, BF16),
            pltpu.VMEM((node_blocks, rows8, block), F32),
            pltpu.VMEM((panel_blocks, rows8, block), F32),
            pltpu.SMEM(pair_struct.shape, jnp.int32),
            pltpu.SMEM(pair_panel.shape, jnp.int32),
            pltpu.SemaphoreType.DMA((slots // FORWARD_GROUP,)),
            pltpu.SemaphoreType.DMA((3,)),
            pltpu.SemaphoreType.DMA,
        ],
        compiler_params=pltpu.CompilerParams(vmem_limit_bytes=8 << 20),
    )(pair_count, *[in_hbm(a) for a in
                    (pair_struct, pair_panel, velocity, mortar_coef, bem_matrix)])

    chip = keep + swap(send, "row", nrow, 1)
    plane = chip[0]
    arrived = [swap(chip[k], "col", ncol, k) for k in range(1, ncol)]
    held = fetch_rows(head_rows, window_rows, chip, held, bem_matrix)
    for got in arrived:
        plane = plane + got
    sent = plane.astype(BF16)
    whole = plane
    arrived = [swap(sent, "row", nrow, 2 * k) for k in range(1, nrow // 2)]
    held = fetch_rows(head_rows + window_rows, window_rows, sent, held, bem_matrix)
    for got in arrived:
        whole = whole + got.astype(F32)
    xa = whole.astype(BF16)
    xb = swap(xa, "row", nrow, 1)

    partial_value, _ = pl.pallas_call(
        functools.partial(bem_kernel, (head_rows + 2 * window_rows) // chunk_rows, BODY_CHUNKS),
        name="bem_product",
        out_shape=[
            jax.ShapeDtypeStruct((cases, rows), F32),
            pltpu.VMEM((buffer_rows, width), BF16),
        ],
        in_specs=[vmem, vmem, hbm, vmem, hbm],
        out_specs=[vmem, vmem],
        scratch_shapes=[
            pltpu.VMEM((rows8, width), BF16),
            pltpu.VMEM((rows,), F32),
            pltpu.SemaphoreType.DMA((buffer_rows // chunk_rows,)),
            pltpu.SemaphoreType.DMA,
        ],
        input_output_aliases={3: 1},
        compiler_params=pltpu.CompilerParams(vmem_limit_bytes=8 << 20),
    )(xa, xb, in_hbm(self_term), held, in_hbm(bem_matrix))

    total = partial_value
    for got in [swap(partial_value, "col", ncol, k) for k in range(1, ncol)]:
        total = total + got
    pressure = total.astype(BF16)

    mine = [pressure] + [swap(pressure, "row", nrow, 2 * k) for k in range(1, nrow // 2)]
    pieces = []
    for got in mine:
        pieces.append(got)
        pieces.append(swap(got, "row", nrow, 1))

    load = pl.pallas_call(
        functools.partial(backward_kernel, nrow),
        name="mortar_backward",
        out_shape=jax.ShapeDtypeStruct((cases, node_blocks * wide), F32),
        in_specs=[hbm, hbm, smem, vmem] + [vmem] * nrow,
        out_specs=vmem,
        scratch_shapes=[
            pltpu.VMEM((panel_blocks, rows8, block), F32),
            pltpu.VMEM((node_blocks, rows8, block), F32),
            pltpu.SMEM(pair_struct.shape, jnp.int32),
            pltpu.SMEM(pair_panel.shape, jnp.int32),
            pltpu.SemaphoreType.DMA((2,)),
        ],
        compiler_params=pltpu.CompilerParams(vmem_limit_bytes=8 << 20),
    )(in_hbm(pair_struct), in_hbm(pair_panel), pair_count, coef, *pieces)
    return (pressure, load)


def solution(mesh):
    placed = (
        P(None, ("col", "row")),
        P(("col", "row")),
        P(("col", "row")),
        P(("col", "row")),
        P(("col", "row"), None, None),
        P("row", "col"),
        P("row"),
    )
    return jax.shard_map(
        on_device,
        mesh=mesh,
        in_specs=placed,
        out_specs=(P(None, "row"), P(None, ("col", "row"))),
        check_vma=False,
    )
```

```python
import functools

import jax
import jax.numpy as jnp
from jax import lax
from jax.experimental import pallas as pl
from jax.experimental.pallas import tpu as pltpu
from jax.sharding import PartitionSpec as P


F32 = jnp.float32
BF16 = jnp.bfloat16
FORWARD_GROUP = 32
BACKWARD_GROUP = 128
HEAD_ROWS = 256
WINDOW_ROWS = 384
CHUNK_ROWS = 128
BODY_CHUNKS = 4
BUFFER_ROWS = 1536


def half_split(block, wide):
    src = lax.broadcasted_iota(jnp.int32, (wide, wide), 0)
    dst = lax.broadcasted_iota(jnp.int32, (wide, wide), 1)
    want = jnp.where(dst < block, 2 * dst, 2 * (dst - block) + 1)
    return jnp.where(src == want, 1.0, 0.0).astype(BF16)


def half_spread(block, part):
    src = lax.broadcasted_iota(jnp.int32, (block, 2 * block), 0)
    dst = lax.broadcasted_iota(jnp.int32, (block, 2 * block), 1)
    return jnp.where(dst == 2 * src + part, 1.0, 0.0).astype(BF16)


def unpack_parts(wide_rows, cases, block):
    nb = wide_rows.shape[0]
    both = jnp.concatenate([wide_rows, wide_rows], axis=1)
    flat = both.reshape(nb * 2 * cases, 2 * block).astype(BF16)
    out = jnp.dot(flat, half_split(block, 2 * block), preferred_element_type=F32)
    out = out.reshape(nb, 2 * cases, 2 * block)
    row = lax.broadcasted_iota(jnp.int32, (nb, 2 * cases, block), 1)
    return jnp.where(row < cases, out[:, :, :block], out[:, :, block:])


def forward_kernel(head_rows, count_ref, struct_hbm, panel_hbm, vel_hbm, coef_hbm, bem_hbm,
                   keep_ref, send_ref, head_ref, coef,
                   vel_ref, vel, acc, struct_ref, panel_ref,
                   sems, small_sems, head_sem):
    slots, block, _ = coef.shape
    cases = vel_ref.shape[0]
    nblk = vel.shape[0]
    chunks = slots // FORWARD_GROUP
    core = lax.rem(lax.axis_index("row"), 2)

    def fetch(i):
        part = pl.ds(i * FORWARD_GROUP, FORWARD_GROUP)
        return pltpu.make_async_copy(coef_hbm.at[part], coef.at[part], sems.at[i])

    small = [
        pltpu.make_async_copy(src, dst, small_sems.at[n])
        for n, (src, dst) in enumerate(
            [(vel_hbm, vel_ref), (struct_hbm, struct_ref), (panel_hbm, panel_ref)])
    ]
    head_copy = pltpu.make_async_copy(
        bem_hbm.at[pl.ds(0, head_rows)], head_ref.at[pl.ds(0, head_rows)], head_sem)
    for copy in small:
        copy.start()
    for i in range(chunks):
        fetch(i).start()
    head_copy.start()
    acc[...] = jnp.zeros_like(acc)
    wide = 2 * block
    small[0].wait()
    rows = jnp.stack(
        [vel_ref[:, b * wide:(b + 1) * wide].astype(F32) for b in range(nblk)], axis=0
    )
    vel[...] = unpack_parts(rows, cases, block)
    for copy in small[1:]:
        copy.wait()
    count = count_ref[0]
    zero = jnp.zeros((2 * cases, block), F32)

    def group(i, carry):
        fetch(i).wait()
        base = i * FORWARD_GROUP
        outs = []
        for j in range(0, FORWARD_GROUP, 2):
            qa, qb = base + j, base + j + 1
            va = jnp.where(qa < count, vel[struct_ref[qa]], 0.0)
            vb = jnp.where(qb < count, vel[struct_ref[qb]], 0.0)
            lhs = jnp.concatenate(
                [jnp.concatenate([va, zero], axis=1), jnp.concatenate([zero, vb], axis=1)], axis=0
            ).astype(BF16)
            rhs = jnp.concatenate([coef[qa], coef[qb]], axis=1)
            outs.append(lax.dot_general(lhs, rhs, (((1,), (1,)), ((), ())),
                                        preferred_element_type=F32))
        for j in range(0, FORWARD_GROUP, 2):
            out = outs[j // 2]
            acc[panel_ref[base + j]] += out[:2 * cases]
            acc[panel_ref[base + j + 1]] += out[2 * cases:]
        return carry

    lax.fori_loop(0, chunks, group, 0)
    cols, half = keep_ref.shape[0], keep_ref.shape[1]
    for k in range(cols):
        c = lax.axis_index("col") ^ k
        keep_ref[k] = acc[pl.ds((2 * c + core) * half, half)]
        send_ref[k] = acc[pl.ds((2 * c + 1 - core) * half, half)]
    head_copy.wait()


def fetch_kernel(start, count, after_ref, held_ref, bem_hbm, out_ref, sem):
    part = pl.ds(start, count)
    copy = pltpu.make_async_copy(bem_hbm.at[part], out_ref.at[part], sem)
    copy.start()
    copy.wait()


def fetch_rows(start, count, after, held, bem_matrix):
    hbm = pl.BlockSpec(memory_space=pl.ANY)
    vmem = pl.BlockSpec(memory_space=pltpu.VMEM)
    return pl.pallas_call(
        functools.partial(fetch_kernel, start, count),
        name="fetch_rows",
        out_shape=pltpu.VMEM(held.shape, BF16),
        in_specs=[hbm, vmem, hbm],
        out_specs=vmem,
        scratch_shapes=[pltpu.SemaphoreType.DMA],
        input_output_aliases={1: 0},
        compiler_params=pltpu.CompilerParams(vmem_limit_bytes=1 << 20),
        cost_estimate=pl.CostEstimate(
            flops=0, transcendentals=0, bytes_accessed=2 * count * held.shape[1]),
    )(after, held, in_hbm(bem_matrix))


def bem_kernel(ready, per, xa_ref, xb_ref, self_hbm, held_ref, bem_hbm, out_ref, tiles,
               xrow, self_ref, sems, self_sem):
    half, rows8, block = xa_ref.shape
    cases = rows8 // 2
    rows, width = bem_hbm.shape
    ring = sems.shape[0]
    chunk = tiles.shape[0] // ring
    chunks = rows // chunk
    tile = per * chunk
    row_id = lax.axis_index("row")
    core = lax.rem(row_id, 2)
    wide = 2 * block

    def fetch(i):
        slot = lax.rem(i, ring)
        to = pl.ds(pl.multiple_of(slot * chunk, chunk), chunk)
        return pltpu.make_async_copy(
            bem_hbm.at[pl.ds(pl.multiple_of(i * chunk, chunk), chunk)], tiles.at[to],
            sems.at[slot])

    self_copy = pltpu.make_async_copy(self_hbm, self_ref, self_sem)
    for i in range(ready, min(ready + 1, ring, chunks)):
        fetch(i).start()
    parts = jnp.concatenate([xa_ref[...], xb_ref[...]], axis=0).astype(F32)
    flat = parts.reshape(2 * half * rows8, block).astype(BF16)
    even = jnp.dot(flat, half_spread(block, 0), preferred_element_type=F32)
    odd = jnp.dot(flat, half_spread(block, 1), preferred_element_type=F32)
    line = lax.broadcasted_iota(jnp.int32, even.shape, 0)
    both = jnp.where(lax.rem(line, rows8) < cases, even, odd)
    both = both.reshape(2 * half, rows8, wide)
    for j in range(half):
        first = jnp.where(core == 0, both[j], both[half + j])
        second = jnp.where(core == 0, both[half + j], both[j])
        xrow[:, j * wide:(j + 1) * wide] = first.astype(BF16)
        xrow[:, (half + j) * wide:(half + j + 1) * wide] = second.astype(BF16)

    for i in range(ready + 1, min(ring, chunks)):
        fetch(i).start()
    self_copy.start()

    def step(i, carry):
        for n in range(per):
            @pl.when(i * per + n >= ready)
            def _(n=n):
                fetch(i * per + n).wait()

            @pl.when(jnp.logical_and(i >= 1, (i - 1) * per + n + ring < chunks))
            def _(n=n):
                fetch((i - 1) * per + n + ring).start()

        slot = lax.rem(i, ring // per)
        got = lax.dot_general(
            xrow[...], tiles[pl.ds(pl.multiple_of(slot * tile, tile), tile)],
            (((1,), (1,)), ((), ())), preferred_element_type=F32)
        out_ref[:, pl.ds(pl.multiple_of(i * tile, tile), tile)] = got[:cases] + got[cases:]
        return carry

    lax.fori_loop(0, chunks // per, step, 0)
    start = row_id * rows
    self_copy.wait()

    @pl.when(start // width == lax.axis_index("col"))
    def _():
        offset = pl.multiple_of(lax.rem(start, width), rows)
        own = xrow[:, pl.ds(offset, rows)].astype(F32)
        out_ref[...] += self_ref[...][None, :] * (own[:cases] + own[cases:])


def backward_kernel(ranks, struct_hbm, panel_hbm, count_ref, coef, *refs):
    pieces, scratch = refs[:ranks], refs[ranks:]
    out_ref, table, acc, struct_ref, panel_ref, sems = scratch
    small = [
        pltpu.make_async_copy(src, dst, sems.at[n])
        for n, (src, dst) in enumerate(
            [(struct_hbm, struct_ref), (panel_hbm, panel_ref)])
    ]
    for copy in small:
        copy.start()
    slots, block, _ = coef.shape
    nblk, rows8, _ = acc.shape
    cases = rows8 // 2
    wide = 2 * block
    me = lax.axis_index("row")
    per = pieces[0].shape[1] // wide
    for k in range(ranks):
        rows = jnp.stack(
            [pieces[k][:, b * wide:(b + 1) * wide].astype(F32) for b in range(per)], axis=0)
        table[pl.ds((me ^ k) * per, per)] = unpack_parts(rows, cases, block)
    acc[...] = jnp.zeros_like(acc)
    for copy in small:
        copy.wait()
    count = count_ref[0]

    def group(i, carry):
        base = i * BACKWARD_GROUP
        outs = []
        for j in range(0, BACKWARD_GROUP, 2):
            qa, qb = base + j, base + j + 1
            pa = jnp.where(qa < count, table[panel_ref[qa]], 0.0)
            pb = jnp.where(qb < count, table[panel_ref[qb]], 0.0)
            lhs = jnp.concatenate([pa, pb], axis=0).astype(BF16)
            rhs = jnp.concatenate([coef[qa], coef[qb]], axis=1)
            outs.append(jnp.dot(lhs, rhs, preferred_element_type=F32))
        for j in range(0, BACKWARD_GROUP, 2):
            out = outs[j // 2]
            acc[struct_ref[base + j]] += out[:rows8, :block]
            acc[struct_ref[base + j + 1]] += out[rows8:, block:]
        return carry

    lax.fori_loop(0, slots // BACKWARD_GROUP, group, 0)
    rest = acc[...].reshape(nblk * rows8, block)
    even = odd = None
    spread0, spread1 = half_spread(block, 0), half_spread(block, 1)
    for _ in range(2):
        piece = rest.astype(BF16)
        rest = rest - piece.astype(F32)
        e = jnp.dot(piece, spread0, preferred_element_type=F32)
        o = jnp.dot(piece, spread1, preferred_element_type=F32)
        even = e if even is None else even + e
        odd = o if odd is None else odd + o
    even = even.reshape(nblk, rows8, wide)
    odd = odd.reshape(nblk, rows8, wide)
    for b in range(nblk):
        out_ref[:, b * wide:(b + 1) * wide] = even[b, :cases] + odd[b, cases:]


def swap(value, axis, size, mask):
    return lax.ppermute(value, axis, [(i, i ^ mask) for i in range(size)])


def in_hbm(value):
    return pltpu.with_memory_space_constraint(value, pltpu.HBM)


def on_device(velocity, pair_struct, pair_panel, pair_count, mortar_coef, bem_matrix, self_term):
    cases = velocity.shape[0]
    slots, block, _ = mortar_coef.shape
    wide = 2 * block
    node_blocks = velocity.shape[1] // wide
    ncol, nrow = lax.axis_size("col"), lax.axis_size("row")
    rows, width = bem_matrix.shape
    panel_blocks = ncol * width // wide
    half = panel_blocks // (2 * ncol)
    rows8 = 2 * cases
    smem = pl.BlockSpec(memory_space=pltpu.SMEM)
    vmem = pl.BlockSpec(memory_space=pltpu.VMEM)
    hbm = pl.BlockSpec(memory_space=pl.ANY)

    head_rows = min(HEAD_ROWS, rows // 4)
    window_rows = min(WINDOW_ROWS, rows // 4)
    chunk_rows = min(CHUNK_ROWS, rows // 4)
    buffer_rows = min(BUFFER_ROWS, rows)
    keep, send, held, coef = pl.pallas_call(
        functools.partial(forward_kernel, head_rows),
        name="mortar_forward",
        out_shape=[
            jax.ShapeDtypeStruct((ncol, half, rows8, block), F32),
            jax.ShapeDtypeStruct((ncol, half, rows8, block), F32),
            pltpu.VMEM((buffer_rows, width), BF16),
            pltpu.VMEM(mortar_coef.shape, BF16),
        ],
        in_specs=[smem] + [hbm] * 5,
        out_specs=[vmem] * 4,
        scratch_shapes=[
            pltpu.VMEM(velocity.shape, BF16),
            pltpu.VMEM((node_blocks, rows8, block), F32),
            pltpu.VMEM((panel_blocks, rows8, block), F32),
            pltpu.SMEM(pair_struct.shape, jnp.int32),
            pltpu.SMEM(pair_panel.shape, jnp.int32),
            pltpu.SemaphoreType.DMA((slots // FORWARD_GROUP,)),
            pltpu.SemaphoreType.DMA((3,)),
            pltpu.SemaphoreType.DMA,
        ],
        compiler_params=pltpu.CompilerParams(vmem_limit_bytes=8 << 20),
    )(pair_count, *[in_hbm(a) for a in
                    (pair_struct, pair_panel, velocity, mortar_coef, bem_matrix)])

    chip = keep + swap(send, "row", nrow, 1)
    plane = chip[0]
    arrived = [swap(chip[k], "col", ncol, k) for k in range(1, ncol)]
    held = fetch_rows(head_rows, window_rows, chip, held, bem_matrix)
    for got in arrived:
        plane = plane + got
    sent = plane.astype(BF16)
    whole = plane
    arrived = [swap(sent, "row", nrow, 2 * k) for k in range(1, nrow // 2)]
    held = fetch_rows(head_rows + window_rows, window_rows, sent, held, bem_matrix)
    for got in arrived:
        whole = whole + got.astype(F32)
    xa = whole.astype(BF16)
    xb = swap(xa, "row", nrow, 1)

    partial_value, _ = pl.pallas_call(
        functools.partial(bem_kernel, (head_rows + 2 * window_rows) // chunk_rows, BODY_CHUNKS),
        name="bem_product",
        out_shape=[
            jax.ShapeDtypeStruct((cases, rows), F32),
            pltpu.VMEM((buffer_rows, width), BF16),
        ],
        in_specs=[vmem, vmem, hbm, vmem, hbm],
        out_specs=[vmem, vmem],
        scratch_shapes=[
            pltpu.VMEM((rows8, width), BF16),
            pltpu.VMEM((rows,), F32),
            pltpu.SemaphoreType.DMA((buffer_rows // chunk_rows,)),
            pltpu.SemaphoreType.DMA,
        ],
        input_output_aliases={3: 1},
        compiler_params=pltpu.CompilerParams(vmem_limit_bytes=8 << 20),
    )(xa, xb, in_hbm(self_term), held, in_hbm(bem_matrix))

    total = partial_value
    for got in [swap(partial_value, "col", ncol, k) for k in range(1, ncol)]:
        total = total + got
    pressure = total.astype(BF16)

    mine = [pressure] + [swap(pressure, "row", nrow, 2 * k) for k in range(1, nrow // 2)]
    pieces = []
    for got in mine:
        pieces.append(got)
        pieces.append(swap(got, "row", nrow, 1))

    load = pl.pallas_call(
        functools.partial(backward_kernel, nrow),
        name="mortar_backward",
        out_shape=jax.ShapeDtypeStruct((cases, node_blocks * wide), F32),
        in_specs=[hbm, hbm, smem, vmem] + [vmem] * nrow,
        out_specs=vmem,
        scratch_shapes=[
            pltpu.VMEM((panel_blocks, rows8, block), F32),
            pltpu.VMEM((node_blocks, rows8, block), F32),
            pltpu.SMEM(pair_struct.shape, jnp.int32),
            pltpu.SMEM(pair_panel.shape, jnp.int32),
            pltpu.SemaphoreType.DMA((2,)),
        ],
        compiler_params=pltpu.CompilerParams(vmem_limit_bytes=8 << 20),
    )(in_hbm(pair_struct), in_hbm(pair_panel), pair_count, coef, *pieces)
    return (pressure, load)


def solution(mesh):
    placed = (
        P(None, ("col", "row")),
        P(("col", "row")),
        P(("col", "row")),
        P(("col", "row")),
        P(("col", "row"), None, None),
        P("row", "col"),
        P("row"),
    )
    return jax.shard_map(
        on_device,
        mesh=mesh,
        in_specs=placed,
        out_specs=(P(None, "row"), P(None, ("col", "row"))),
        check_vma=False,
    )
```
